128 devices in a mesh: dp: 8 (over z_hi, x), land: 16 (over z_lo, y, core).
Axes of the slice: x: 4, y: 4, z: 4 (z_hi: 2, z_lo: 2; z = z_hi * 2 + z_lo), core: 2. Of those that a mesh axis runs over, the one named last changes fastest.
Arguments:
- items: bfloat16 [65536, 768], P(('dp', 'land')), may hold values from -1.5 to 1.5
- landmarks: bfloat16 [16384, 768], P('land'), may hold values from -1.5 to 1.5
- scales: float32 [16384], P('land'), may hold values from 0.25 to 1
- eigvecs: bfloat16 [16384, 256], P('land'), may hold values from -0.046875 to 0.046875
- eigvals: float32 [256], replicated, may hold values from 0.5 to 2
Outputs:
- coords: float32 [65536, 256], P(('dp', 'land'))
- gram: float32 [256, 256], replicated
The draws below stay inside these ranges and needn't reach their ends.
All inputs are finite; a program needn't handle non-finite values.
Results may differ from the reference program's by a relative error of at most 0.0028.
Values may be sent and summed in bfloat16 or wider, within the bound.
A program may use at most 128 MiB of HBM per device.

```python
import math
import jax
import jax.numpy as jnp
from jax import lax

D = 768
K = 256
LAND_DEV = 1024
ROW_DEV = 512
LANDMARKS = 16384
NROWS = 65536
N_LAND = 16


latent_dims = 16


def shared_basis(key):
    basis = jax.random.normal(jax.random.fold_in(key, 7), (D, latent_dims), jnp.float32)
    basis = jnp.clip(basis, -4.0, 4.0) / jnp.sqrt(jnp.float32(D))
    return basis


def base_latent(key, count, salt):
    latent = jnp.clip(jax.random.normal(jax.random.fold_in(key, salt), (count, latent_dims), jnp.float32), -4.0, 4.0)
    noise = jnp.clip(jax.random.normal(jax.random.fold_in(key, salt + 1), (count, D), jnp.float32), -4.0, 4.0)
    return (latent, noise)


def embed_points(key, latent, noise):
    spread = jnp.sqrt(jnp.float32(3.0 / latent_dims))
    values = jnp.dot(latent * spread, shared_basis(key).T, precision=lax.Precision.HIGHEST)
    values = values + noise * jnp.sqrt(jnp.float32(0.25) / jnp.float32(D))
    return jnp.clip(values, -1.5, 1.5).astype(jnp.bfloat16)


def block_layout(key):
    block_count = NROWS // ROW_DEV
    land_count = LANDMARKS // LAND_DEV
    group_count = block_count // land_count
    block_ids = jnp.arange(block_count)
    group_pos = ((block_ids // land_count).astype(jnp.float32) + 0.5) / jnp.float32(group_count) - 0.5
    land_pos = ((block_ids % land_count).astype(jnp.float32) + 0.5) / jnp.float32(land_count) - 0.5
    signs = jnp.where(jax.random.uniform(jax.random.fold_in(key, 41), (2,), jnp.float32) < 0.5, -1.0, 1.0)
    jitter = jax.random.uniform(jax.random.fold_in(key, 43), (block_count,), jnp.float32, -0.25, 0.25)
    log_scale = 0.7 * signs[0] * group_pos + 0.4 * signs[1] * land_pos + jitter
    directions = jax.random.normal(jax.random.fold_in(key, 45), (2, latent_dims), jnp.float32)
    directions = directions / jnp.sqrt(jnp.sum(directions * directions, axis=1, keepdims=True))
    wobble = jnp.clip(jax.random.normal(jax.random.fold_in(key, 47), (block_count, latent_dims), jnp.float32), -4.0, 4.0)
    offsets = 3.0 * group_pos[:, None] * directions[0][None, :] + 2.0 * land_pos[:, None] * directions[1][None, :] + 0.25 * wobble
    return (jnp.exp(log_scale), offsets)


def draw_items(key, part):
    latent, noise = base_latent(key, NROWS, 21)
    stretch, offsets = block_layout(key)
    block_count = NROWS // ROW_DEV
    latent = latent.reshape(block_count, ROW_DEV, latent_dims) * stretch[:, None, None] + offsets[:, None, :]
    return embed_points(key, latent.reshape(NROWS, latent_dims), noise)


def draw_landmarks(key, part):
    latent, noise = base_latent(key, LANDMARKS, 31)
    return embed_points(key, latent * 1.3, noise)


def block_levels(own_key, dims, shards, low, high):
    factor_of, own = 1.0, jax.random.fold_in(own_key, 6)
    for position, blocks in shards:
        draws = jnp.exp(jax.random.uniform(jax.random.fold_in(own, position), (blocks,), jnp.float32, low / len(shards), high / len(shards)))
        factor_of = factor_of * jnp.repeat(draws, dims[position] // blocks).reshape([-1 if axis == position else 1 for axis in range(len(dims))])
    return factor_of


def normal_values(own_key, extent, scale, limit, shards=(), held_as=jnp.bfloat16):
    entries = scale * jax.random.normal(own_key, extent, jnp.float32)
    if shards:
        entries = entries * block_levels(own_key, extent, shards, -0.22, 0.18)
    return jnp.clip(entries, -limit, limit).astype(held_as)


def setup_inputs(seed: int = 0) -> dict:
    key_list = jax.random.split(jax.random.key(seed), 6)
    return {
        "items": draw_items(jax.random.fold_in(key_list[5], 71), 0),
        "landmarks": draw_landmarks(jax.random.fold_in(key_list[5], 71), 0),
        "scales": jnp.clip(jnp.exp(math.log(1.0) - 1.3862944 * jax.random.uniform(key_list[2], (LANDMARKS,), jnp.float32) ** block_levels(key_list[2], (LANDMARKS,), ((0, 16),), -0.2, 0.2)), 0.25, 1.0),
        "eigvecs": normal_values(key_list[3], (LANDMARKS, K), LANDMARKS ** -0.5, 0.046875, ((0, 16),)),
        "eigvals": jnp.clip(jnp.exp(jax.random.uniform(key_list[4], (K,), jnp.float32, math.log(0.5), math.log(2.0))), 0.5, 2.0),
    }


def kernel_block(rows, landmarks, scales):
    row_vals = rows.astype(jnp.float32)
    land_vals = landmarks.astype(jnp.float32)
    row_sq = lax.optimization_barrier(jnp.sum(row_vals * row_vals, axis=1))
    land_sq = lax.optimization_barrier(jnp.sum(land_vals * land_vals, axis=1))
    cross = jnp.dot(rows, landmarks.T, preferred_element_type=jnp.float32)
    dist = row_sq[:, None] + land_sq[None, :] - 2.0 * cross
    return jnp.exp(-dist * scales[None, :])

def reference(items, landmarks, scales, eigvecs, eigvals):
    group = ROW_DEV * N_LAND
    blocks = items.reshape(NROWS // group, group, D)

    def first_pass(rows):
        kernel = kernel_block(rows, landmarks, scales)
        return (lax.optimization_barrier(jnp.sum(kernel, axis=0)), lax.optimization_barrier(jnp.sum(kernel, axis=1)))
    land_parts, row_degree = lax.map(first_pass, blocks)
    land_degree = lax.optimization_barrier(jnp.sum(land_parts, axis=0))
    factor = jnp.sqrt(jnp.float32(NROWS) * jnp.float32(LANDMARKS))

    def second_pass(inputs):
        rows, degrees = inputs
        kernel = kernel_block(rows, landmarks, scales)
        scaled = (kernel / jnp.sqrt(land_degree)[None, :]).astype(jnp.bfloat16)
        partial_value = jnp.dot(scaled, eigvecs, preferred_element_type=jnp.float32)
        coords = partial_value * (factor / jnp.sqrt(degrees))[:, None] / eigvals[None, :]
        outer = jnp.dot(coords.T, coords, precision=lax.Precision.HIGHEST)
        return (coords, outer)
    coords, outers = lax.map(second_pass, (blocks, row_degree))
    gram = lax.optimization_barrier(jnp.sum(outers, axis=0)) / jnp.float32(NROWS)
    return (coords.reshape(NROWS, K), gram)
```

```python
import jax
import jax.numpy as jnp
from jax import lax
from jax.experimental import pallas as pl
from jax.experimental.pallas import tpu as pltpu
from jax.sharding import PartitionSpec as P


f32, bf16 = jnp.float32, jnp.bfloat16
LOG2E = 1.4426950408889634
OWN, NEAR, NEXT, FAR = 0, 1, 2, 3
NX = NY = NZ = 4
GROUP = 8


def place(x, y, z, c):
    return {"dp": lax.div(z, 2) * NX + x, "land": lax.rem(z, 2) * 8 + y * 2 + c}


def kernel(items, lands, vecs, scales, eigvals, coords, gram,
           it, lmk, evs, lp, rh, kmat, rowacc, colacc, cross,
           ldx, ldz, rsv, degs, degr, scl, acc, psend, precv,
           gpart, grx, gry, grz, gfull,
           loc, ssem, rsem, gs, gr, bar_unused):
    rows, halfr = items.shape[0], items.shape[0] // 2
    nl = lands.shape[0]
    halfl = nl // 2
    dp, land = lax.axis_index("dp"), lax.axis_index("land")
    x, zh = lax.rem(dp, NX), lax.div(dp, NX)
    c, y, zl = lax.rem(land, 2), lax.rem(lax.div(land, 2), NY), lax.div(land, 8)
    z = zh * 2 + zl
    yn, yp = lax.rem(y + 1, NY), lax.rem(y + NY - 1, NY)
    zn, zp = lax.rem(z + 1, NZ), lax.rem(z + NZ - 1, NZ)
    yfar = lax.rem(y + 2, NY)
    up, down, far = place(x, yn, z, c), place(x, yp, z, c), place(x, yfar, z, c)
    zup, zdown = place(x, y, zn, c), place(x, y, zp, c)
    sib = place(x, y, z, 1 - c)
    g = x * 2 + c
    group = []
    for k in range(1, GROUP):
        p = lax.rem(g + k, GROUP)
        group.append((p, place(lax.div(p, 2), y, z, lax.rem(p, 2))))
    zline = [(lax.rem(z + k, NZ), place(x, y, lax.rem(z + k, NZ), c)) for k in range(1, NZ)]
    yline = [(lax.rem(y + k, NY), place(x, lax.rem(y + k, NY), z, c)) for k in range(1, NY)]
    q = zl * 2 + c
    q_sib, q_oth, q_osib = zl * 2 + 1 - c, (1 - zl) * 2 + c, (1 - zl) * 2 + 1 - c

    barrier = pltpu.get_barrier_semaphore()
    peers = [d for _, d in group] + [d for _, d in zline] + [d for _, d in yline]
    for d in peers:
        pl.semaphore_signal(barrier, inc=1, device_id=d, device_id_type=pl.DeviceIdType.MESH)

    own_i = pltpu.make_async_copy(items, it.at[OWN], loc.at[0])
    own_l = pltpu.make_async_copy(lands, lmk.at[q], loc.at[1])
    own_v = pltpu.make_async_copy(vecs, evs.at[q], loc.at[2])
    own_l.start()
    own_i.start()
    own_v.start()

    pl.semaphore_wait(barrier, len(peers))

    sends = []

    def rc(i, src, dst, d):
        return pltpu.make_async_remote_copy(
            src_ref=src, dst_ref=dst, send_sem=ssem.at[i], recv_sem=rsem.at[i],
            device_id=d, device_id_type=pl.DeviceIdType.MESH)

    def go(cp):
        cp.start()
        sends.append(cp)

    lo, hi = pl.ds(0, halfr), pl.ds(halfr, halfr)
    llo, lhi = pl.ds(0, halfl), pl.ds(halfl, halfl)
    i0 = rc(0, items.at[lo], it.at[NEAR, lo], up)
    i1 = rc(1, items.at[hi], it.at[NEAR, hi], down)
    i2 = rc(2, items.at[hi], it.at[NEXT, lo], up)
    i3 = rc(3, items.at[lo], it.at[NEXT, hi], down)
    i4 = rc(4, it.at[NEAR, lo], it.at[FAR, lo], up)
    i5 = rc(5, it.at[NEAR, hi], it.at[FAR, hi], down)
    l0 = rc(6, lands, lmk.at[q], sib)
    l1 = rc(7, lands.at[llo], lmk.at[q, llo], zup)
    l2 = rc(8, lands.at[lhi], lmk.at[q, lhi], zdown)
    l1r = rc(7, lands.at[llo], lmk.at[q_oth, llo], zup)
    l2r = rc(8, lands.at[lhi], lmk.at[q_oth, lhi], zdown)
    l0r = rc(6, lands, lmk.at[q_sib], sib)
    l3 = rc(9, lmk.at[q_oth, llo], lmk.at[q_oth, llo], sib)
    l4 = rc(10, lmk.at[q_oth, lhi], lmk.at[q_oth, lhi], sib)
    l3r = rc(9, lmk.at[q_oth, llo], lmk.at[q_osib, llo], sib)
    l4r = rc(10, lmk.at[q_oth, lhi], lmk.at[q_osib, lhi], sib)
    p0 = rc(11, lp.at[q], lp.at[q], sib)
    p0r = rc(11, lp.at[q], lp.at[q_sib], sib)
    p1 = rc(12, lp.at[q], lp.at[q], zup)
    p1r = rc(12, lp.at[q], lp.at[q_oth], zup)
    p2 = rc(13, lp.at[q_oth], lp.at[q_oth], sib)
    p2r = rc(13, lp.at[q_oth], lp.at[q_osib], sib)
    v0 = rc(14, vecs, evs.at[q], sib)
    v0r = rc(14, vecs, evs.at[q_sib], sib)
    v1 = rc(15, vecs.at[llo], evs.at[q, llo], zup)
    v1r = rc(15, vecs.at[llo], evs.at[q_oth, llo], zup)
    v2 = rc(16, vecs.at[lhi], evs.at[q, lhi], zdown)
    v2r = rc(16, vecs.at[lhi], evs.at[q_oth, lhi], zdown)
    v3 = rc(17, evs.at[q_oth], evs.at[q_oth], sib)
    v3r = rc(17, evs.at[q_oth], evs.at[q_osib], sib)

    go(i0)
    go(i1)
    go(l1)
    go(l2)
    go(l0)
    go(i2)
    go(i3)

    own_l.wait()
    for r in range(0, nl, 128):
        part = None
        for k in range(0, lands.shape[1], 128):
            v = lmk[q, pl.ds(r, 128), pl.ds(k, 128)].astype(f32)
            part = v * v if part is None else part + v * v
        sq = jnp.sum(part.T, axis=0, keepdims=True)
        s = scales[:, pl.ds(r, 128)] * LOG2E
        lp[q, 0:1, pl.ds(r, 128)] = s + s
        lp[q, 1:2, pl.ds(r, 128)] = -s * sq
        lp[q, 2:8, pl.ds(r, 128)] = jnp.zeros((6, 128), f32)
    go(p0)
    go(p1)
    colacc[...] = jnp.zeros_like(colacc)
    rowacc[...] = jnp.zeros_like(rowacc)

    def half_squares(blk):
        for r in range(0, rows, 128):
            part = None
            for k in range(0, items.shape[1], 128):
                v = it[blk, pl.ds(r, 128), pl.ds(k, 128)].astype(f32)
                part = v * v if part is None else part + v * v
            rh[blk, pl.ds(r, 128), :] = jnp.broadcast_to(0.5 * jnp.sum(part, axis=1, keepdims=True), (128, 128))

    NT, RC = 256, 64

    def block(blk, slot):
        for n in range(0, nl, NT):
            buf = (n // NT) % 2
            cross[buf] = lax.dot_general(
                it[blk], lmk[slot, pl.ds(n, NT), :], (((1,), (1,)), ((), ())), preferred_element_type=f32)
            for w in range(0, NT, 128):
                a = jnp.broadcast_to(lp[slot, 0:1, pl.ds(n + w, 128)], (RC, 128))
                b = jnp.broadcast_to(lp[slot, 1:2, pl.ds(n + w, 128)], (RC, 128))
                col = None
                for r in range(0, rows, RC):
                    t = (cross[buf, pl.ds(r, RC), pl.ds(w, 128)] - rh[blk, pl.ds(r, RC), :]) * a + b
                    kv = jnp.exp2(t)
                    kmat[blk, slot, pl.ds(r, RC), pl.ds(n + w, 128)] = kv
                    rowacc[blk, pl.ds(r, RC), :] += kv
                    ks = jnp.sum(kv.reshape(RC // 8, 8, 128), axis=0)
                    col = ks if col is None else col + ks
                colacc[slot, :, pl.ds(n + w, 128)] += col

    def blocks(pairs):
        n = len(pairs)

        def pick(t, values):
            out = values[-1]
            for i in range(n - 2, -1, -1):
                out = jnp.where(t == i, values[i], out)
            return out

        @pl.loop(0, n)
        def _(t):
            block(pick(t, [jnp.int32(b) for b, _ in pairs]), pick(t, [s for _, s in pairs]))

    own_i.wait()
    half_squares(OWN)
    blocks([(OWN, q)])
    l0r.wait_recv()
    p0r.wait_recv()
    blocks([(OWN, q_sib)])
    i0.wait_recv()
    go(i4)
    i1.wait_recv()
    go(i5)
    half_squares(NEAR)
    blocks([(NEAR, q), (NEAR, q_sib)])
    l1r.wait_recv()
    go(l3)
    l2r.wait_recv()
    go(l4)
    p1r.wait_recv()
    go(p2)
    go(v1)
    go(v2)
    go(v0)
    blocks([(OWN, q_oth), (NEAR, q_oth)])
    i2.wait_recv()
    i3.wait_recv()
    half_squares(NEXT)
    blocks([(NEXT, q), (NEXT, q_sib), (NEXT, q_oth)])
    l3r.wait_recv()
    l4r.wait_recv()
    p2r.wait_recv()
    blocks([(OWN, q_osib), (NEAR, q_osib), (NEXT, q_osib)])
    own_v.wait()
    v1r.wait_recv()
    v2r.wait_recv()
    go(v3)
    i4.wait_recv()
    i5.wait_recv()
    half_squares(FAR)
    blocks([(FAR, q), (FAR, q_sib), (FAR, q_oth), (FAR, q_osib)])

    def gather(buf, me, others, base, n=1):
        for i, (_, d) in enumerate(others):
            go(pltpu.make_async_remote_copy(
                src_ref=buf.at[me], dst_ref=buf.at[me], send_sem=gs.at[base + i], recv_sem=gr.at[base + me],
                device_id=d, device_id_type=pl.DeviceIdType.MESH))
        for p, d in others:
            pltpu.make_async_remote_copy(
                src_ref=buf.at[me], dst_ref=buf.at[p], send_sem=gs.at[base], recv_sem=gr.at[base + p],
                device_id=d, device_id_type=pl.DeviceIdType.MESH).wait_recv()

    for s in range(4):
        ldx[g, :, pl.ds(s * nl, nl)] = jnp.sum(colacc[s], axis=0, keepdims=True)
    gather(ldx, g, group, 0)
    tot = ldx[0]
    for k in range(1, GROUP):
        tot = tot + ldx[k]
    ldz[z] = tot
    gather(ldz, z, zline, 8)
    tot = ldz[0]
    for k in range(1, NZ):
        tot = tot + ldz[k]
    rsv[...] = lax.rsqrt(tot)
    for blk in range(4):
        for h in range(2):
            t = rowacc[blk, pl.ds(h * halfr, halfr), :].T
            degs[blk, h:h + 1, :] = jnp.sum(t, axis=0, keepdims=True)
    dsrc = [
        (degs.at[NEAR, pl.ds(0, 1)], 0, 0, down), (degs.at[NEAR, pl.ds(1, 1)], 1, 1, up),
        (degs.at[NEXT, pl.ds(0, 1)], 0, 1, down), (degs.at[NEXT, pl.ds(1, 1)], 1, 0, up),
        (degs.at[FAR, pl.ds(0, 1)], 2, 0, far), (degs.at[FAR, pl.ds(1, 1)], 2, 1, far)]
    dcp = []
    for i, (src, slot, h, d) in enumerate(dsrc):
        dcp.append(rc(18 + i, src, degr.at[slot, pl.ds(h, 1)], d))
        go(dcp[-1])

    v0r.wait_recv()
    v3r.wait_recv()

    def product(blk):
        acc[...] = jnp.zeros_like(acc)

        @pl.loop(0, 4)
        def _(s):
            part = None
            for k in range(0, nl, 256):
                for w in range(k, k + 256, 128):
                    off = pl.multiple_of(s * nl + w, 128)
                    rv = jnp.broadcast_to(rsv[:, pl.ds(off, 128)], (RC, 128))
                    for r in range(0, rows, RC):
                        scl[pl.ds(r, RC), pl.ds(w, 128)] = (kmat[blk, s, pl.ds(r, RC), pl.ds(w, 128)] * rv).astype(bf16)
                d = jnp.dot(scl[:, pl.ds(k, 256)], evs[s, pl.ds(k, 256), :], preferred_element_type=f32)
                part = d if part is None else part + d
            acc[...] += part

    product(FAR)
    psend[0] = acc[0:halfr]
    psend[1] = acc[halfr:rows]
    r0 = rc(24, psend.at[0], precv.at[0], up)
    r1 = rc(25, psend.at[1], precv.at[1], down)
    go(r0)
    go(r1)
    product(NEAR)
    psend[2] = acc[0:halfr]
    psend[3] = acc[halfr:rows]
    r2 = rc(26, psend.at[2], precv.at[2], down)
    r3 = rc(27, psend.at[3], precv.at[3], up)
    go(r2)
    go(r3)
    product(NEXT)
    r0.wait_recv()
    psend[4] = acc[halfr:rows] + precv[0]
    r4 = rc(28, psend.at[4], precv.at[4], up)
    go(r4)
    r1.wait_recv()
    psend[5] = acc[0:halfr] + precv[1]
    r5 = rc(29, psend.at[5], precv.at[5], down)
    go(r5)
    product(OWN)

    nrows, nlands = float(NROWS), float(LANDMARKS)
    factor = (nrows * nlands) ** 0.5
    for cp in dcp:
        cp.wait_recv()
    r2.wait_recv()
    r3.wait_recv()
    r4.wait_recv()
    r5.wait_recv()
    inv = 1.0 / eigvals[...]
    for h in range(2):
        deg = degs[OWN, h:h + 1, :]
        for k in range(3):
            deg = deg + degr[k, h:h + 1, :]
        f = factor / jnp.sqrt(deg)
        col = jnp.broadcast_to(f, (128, halfr)).T
        for w in range(0, 256, 128):
            v = acc[pl.ds(h * halfr, halfr), pl.ds(w, 128)] + precv[2 + h, :, pl.ds(w, 128)] + precv[4 + h, :, pl.ds(w, 128)]
            coords[pl.ds(h * halfr, halfr), pl.ds(w, 128)] = v * col * inv[:, w:w + 128]

    cv = coords[...]
    gpart[...] = lax.dot_general(cv, cv, (((0,), (0,)), ((), ())), precision=lax.Precision.HIGHEST,
                                 preferred_element_type=f32).reshape(gpart.shape)
    for i, (p, d) in enumerate(group):
        go(pltpu.make_async_remote_copy(
            src_ref=gpart.at[p], dst_ref=grx.at[g], send_sem=gs.at[12 + i], recv_sem=gr.at[12 + g],
            device_id=d, device_id_type=pl.DeviceIdType.MESH))
    for p, d in group:
        pltpu.make_async_remote_copy(
            src_ref=gpart.at[p], dst_ref=grx.at[p], send_sem=gs.at[12], recv_sem=gr.at[12 + p],
            device_id=d, device_id_type=pl.DeviceIdType.MESH).wait_recv()
    tot = gpart[g]
    for p, _ in group:
        tot = tot + grx[p]
    gry[y] = tot
    gather(gry, y, yline, 20)
    tot = gry[0]
    for k in range(1, NY):
        tot = tot + gry[k]
    grz[z] = tot
    gather(grz, z, zline, 24)
    tot = grz[0]
    for k in range(1, NZ):
        tot = tot + grz[k]
    gfull[g] = tot * (1.0 / NROWS)
    gather(gfull, g, group, 28)
    gram[...] = gfull[...].reshape(gram.shape)

    for cp in sends:
        cp.wait_send()
NROWS, LANDMARKS = 65536, 16384


def per_device(items, landmarks, scales, eigvecs, eigvals):
    rows, dim = items.shape
    nl, width = eigvecs.shape
    half = rows // 2
    anyspec = pl.BlockSpec(memory_space=pl.ANY)
    vspec = pl.BlockSpec(memory_space=pltpu.VMEM)
    V, DMA = pltpu.VMEM, pltpu.SemaphoreType.DMA
    return pl.pallas_call(
        kernel,
        out_shape=(jax.ShapeDtypeStruct((rows, width), f32), jax.ShapeDtypeStruct((width, width), f32)),
        in_specs=[anyspec, anyspec, anyspec, vspec, vspec],
        out_specs=(vspec, vspec),
        scratch_shapes=[
            V((4, rows, dim), bf16), V((4, nl, dim), bf16), V((4, nl, width), bf16), V((4, 8, nl), f32),
            V((4, rows, 128), f32), V((4, 4, rows, nl), f32), V((4, rows, 128), f32), V((4, 8, nl), f32),
            V((2, rows, 256), f32),
            V((GROUP, 1, 4 * nl), f32), V((NZ, 1, 4 * nl), f32), V((1, 4 * nl), f32), V((4, 2, half), f32), V((3, 2, half), f32),
            V((rows, nl), bf16), V((rows, width), f32), V((6, half, width), f32), V((6, half, width), f32),
            V((GROUP, width // GROUP, width), f32), V((GROUP, width // GROUP, width), f32),
            V((NY, width // GROUP, width), f32), V((NZ, width // GROUP, width), f32),
            V((GROUP, width // GROUP, width), f32),
            DMA((3,)), DMA((30,)), DMA((30,)), DMA((36,)), DMA((36,)), DMA((1,)),
        ],
        compiler_params=pltpu.CompilerParams(collective_id=0, has_side_effects=True, vmem_limit_bytes=62 * 2**20),
    )(items, landmarks, eigvecs, scales.reshape(1, nl), eigvals.reshape(1, width))


def solution(mesh):
    return jax.shard_map(
        per_device, mesh=mesh,
        in_specs=(P(("dp", "land"), None), P("land", None), P("land"), P("land", None), P()),
        out_specs=(P(("dp", "land"), None), P()), check_vma=False)
```

```python
import jax
import jax.numpy as jnp
from jax import lax
from jax.experimental import pallas as pl
from jax.experimental.pallas import tpu as pltpu
from jax.sharding import PartitionSpec as P


f32, bf16 = jnp.float32, jnp.bfloat16
LOG2E = 1.4426950408889634
PT = jnp.bfloat16
NTILE = 512
OWN, NEAR, NEXT, FAR = 0, 1, 2, 3
NX = NY = NZ = 4
GROUP = 8


def place(x, y, z, c):
    return {"dp": lax.div(z, 2) * NX + x, "land": lax.rem(z, 2) * 8 + y * 2 + c}


def kernel(items, lands, vecs, scales, eigvals, coords, gram,
           it, lmk, evs, lp, rh, kmat, rowacc, colacc, cross,
           ldx, ldz, rsv, degs, degr, scl, acc, acc2, psend, precv,
           gpart, grx, gry, grz, gfull,
           loc, ssem, rsem, gs, gr):
    rows, halfr = items.shape[0], items.shape[0] // 2
    nl = lands.shape[0]
    halfl = nl // 2
    dp, land = lax.axis_index("dp"), lax.axis_index("land")
    x, zh = lax.rem(dp, NX), lax.div(dp, NX)
    c, y, zl = lax.rem(land, 2), lax.rem(lax.div(land, 2), NY), lax.div(land, 8)
    z = zh * 2 + zl
    yn, yp = lax.rem(y + 1, NY), lax.rem(y + NY - 1, NY)
    zn, zp = lax.rem(z + 1, NZ), lax.rem(z + NZ - 1, NZ)
    yfar = lax.rem(y + 2, NY)
    up, down, far = place(x, yn, z, c), place(x, yp, z, c), place(x, yfar, z, c)
    zup, zdown = place(x, y, zn, c), place(x, y, zp, c)
    sib = place(x, y, z, 1 - c)
    pos = (x, y, z)

    def at(axis, v, core):
        v = [v if k == axis else pos[k] for k in range(3)]
        return place(*v, core)

    groups, lines, mine = [], [], []
    for axis in range(3):
        g = pos[axis] * 2 + c
        mine.append(g)
        groups.append([])
        for k in range(1, GROUP):
            p = lax.rem(g + k, GROUP)
            groups[axis].append((p, at(axis, lax.div(p, 2), lax.rem(p, 2))))
        lines.append([])
        for k in range(1, NX):
            p = lax.rem(pos[axis] + k, NX)
            lines[axis].append((p, at(axis, p, c)))
    q = zl * 2 + c
    q_sib, q_oth, q_osib = zl * 2 + 1 - c, (1 - zl) * 2 + c, (1 - zl) * 2 + 1 - c

    barrier = pltpu.get_barrier_semaphore()
    peers = [sib] + [at(axis, lax.rem(pos[axis] + k, NX), core) for axis in range(3) for k in range(1, NX) for core in (c, 1 - c)]
    for d in peers:
        pl.semaphore_signal(barrier, inc=1, device_id=d, device_id_type=pl.DeviceIdType.MESH)

    own_i = pltpu.make_async_copy(items, it.at[OWN], loc.at[0])
    own_l = pltpu.make_async_copy(lands, lmk.at[q], loc.at[1])
    own_v = pltpu.make_async_copy(vecs, evs.at[q], loc.at[2])
    own_l.start()
    own_i.start()
    own_v.start()

    sends = []

    def rc(i, src, dst, d):
        return pltpu.make_async_remote_copy(
            src_ref=src, dst_ref=dst, send_sem=ssem.at[i], recv_sem=rsem.at[i],
            device_id=d, device_id_type=pl.DeviceIdType.MESH)

    def go(cp):
        cp.start()
        sends.append(cp)

    qr, ql = rows // 4, nl // 4

    def rq(k, n=1):
        return pl.ds(k * qr, n * qr)

    def lq(k):
        return pl.ds(k * ql, ql)

    a_up = [rc(k, items.at[rq(k)], it.at[NEAR, rq(2 * k)], up) for k in range(2)]
    a_dn = [rc(2 + k, items.at[rq(2 + k)], it.at[NEAR, rq(2 * k + 1)], down) for k in range(2)]
    f_up = [rc(4 + k, it.at[NEAR, rq(2 * k)], it.at[FAR, rq(2 * k)], up) for k in range(2)]
    f_dn = [rc(6 + k, it.at[NEAR, rq(2 * k + 1)], it.at[FAR, rq(2 * k + 1)], down) for k in range(2)]
    b_up = [rc(8 + k, items.at[rq(2 + k)], it.at[NEXT, rq(2 * k)], up) for k in range(2)]
    b_dn = [rc(10 + k, items.at[rq(k)], it.at[NEXT, rq(2 * k + 1)], down) for k in range(2)]
    zdev = [zup, zdown, zup, zdown]
    l_z = [rc(12 + k, lands.at[lq(k)], lmk.at[q, lq(k)], zdev[k]) for k in range(4)]
    l_zr = [rc(12 + k, lands.at[lq(k)], lmk.at[q_oth, lq(k)], zdev[k]) for k in range(4)]
    l_f = [rc(16 + k, lmk.at[q_oth, lq(k)], lmk.at[q_oth, lq(k)], sib) for k in range(4)]
    l_fr = [rc(16 + k, lmk.at[q_oth, lq(k)], lmk.at[q_osib, lq(k)], sib) for k in range(4)]
    l0 = rc(20, lands, lmk.at[q], sib)
    l0r = rc(20, lands, lmk.at[q_sib], sib)
    p0 = rc(21, lp.at[q], lp.at[q], sib)
    p0r = rc(21, lp.at[q], lp.at[q_sib], sib)
    p1 = rc(22, lp.at[q], lp.at[q], zup)
    p1r = rc(22, lp.at[q], lp.at[q_oth], zup)
    p2 = rc(23, lp.at[q_oth], lp.at[q_oth], sib)
    p2r = rc(23, lp.at[q_oth], lp.at[q_osib], sib)
    llo, lhi = pl.ds(0, halfl), pl.ds(halfl, halfl)
    v0 = rc(24, vecs, evs.at[q], sib)
    v0r = rc(24, vecs, evs.at[q_sib], sib)
    v1 = rc(25, vecs.at[llo], evs.at[q, llo], zup)
    v1r = rc(25, vecs.at[llo], evs.at[q_oth, llo], zup)
    v2 = rc(26, vecs.at[lhi], evs.at[q, lhi], zdown)
    v2r = rc(26, vecs.at[lhi], evs.at[q_oth, lhi], zdown)
    v3 = rc(27, evs.at[q_oth], evs.at[q_oth], sib)
    v3r = rc(27, evs.at[q_oth], evs.at[q_osib], sib)

    own_l.wait()
    for r in range(0, nl, 128):
        part = None
        for k in range(0, lands.shape[1], 128):
            v = lmk[q, pl.ds(r, 128), pl.ds(k, 128)].astype(f32)
            part = v * v if part is None else part + v * v
        sq = jnp.sum(part.T, axis=0, keepdims=True)
        s = scales[:, pl.ds(r, 128)] * LOG2E
        lp[q, 0:1, pl.ds(r, 128)] = s + s
        lp[q, 1:2, pl.ds(r, 128)] = -s * sq
        lp[q, 2:8, pl.ds(r, 128)] = jnp.zeros((6, 128), f32)

    pl.semaphore_wait(barrier, len(peers))
    for cp in a_up + a_dn:
        go(cp)
    go(p1)
    go(l0)
    go(p0)
    for cp in l_z:
        go(cp)

    colacc[...] = jnp.zeros_like(colacc)
    rowacc[...] = jnp.zeros_like(rowacc)

    def half_squares(blk, r0, n):
        for r in range(r0, r0 + n, 128):
            part = None
            for k in range(0, items.shape[1], 128):
                v = it[blk, pl.ds(r, 128), pl.ds(k, 128)].astype(f32)
                part = v * v if part is None else part + v * v
            rh[blk, pl.ds(r, 128), :] = jnp.broadcast_to(0.5 * jnp.sum(part, axis=1, keepdims=True), (128, 128))

    NT, RC = NTILE, 64

    def block(blk, slot, r0, m, n0, nn):
        for n in range(n0, n0 + nn, NT):
            buf = (n // NT) % 2
            cross[buf, pl.ds(0, m)] = lax.dot_general(
                it[blk, pl.ds(r0, m), :], lmk[slot, pl.ds(n, NT), :], (((1,), (1,)), ((), ())), preferred_element_type=f32)
            col = [None] * (NT // 128)
            for r in range(0, m, RC):
                half_sq = rh[blk, pl.ds(r0 + r, RC), :]
                row = None
                for w in range(NT // 128):
                    cols = pl.ds(n + w * 128, 128)
                    t = (cross[buf, pl.ds(r, RC), pl.ds(w * 128, 128)] - half_sq) * lp[slot, 0:1, cols] + lp[slot, 1:2, cols]
                    kv = jnp.exp2(t)
                    kmat[blk, slot, pl.ds(r0 + r, RC), cols] = kv
                    row = kv if row is None else row + kv
                    ks = jnp.sum(kv.reshape(RC // 8, 8, 128), axis=0)
                    col[w] = ks if col[w] is None else col[w] + ks
                rowacc[blk, pl.ds(r0 + r, RC), :] += row
            for w in range(NT // 128):
                colacc[slot, :, pl.ds(n + w * 128, 128)] += col[w]

    def blocks(blks, slots, r0=0, m=rows, n0=0, nn=nl):
        pairs = [(b, s) for b in blks for s in slots]
        n = len(pairs)

        def pick(t, values):
            out = values[-1]
            for i in range(n - 2, -1, -1):
                out = jnp.where(t == i, values[i], out)
            return out

        @pl.loop(0, n)
        def _(t):
            block(pick(t, [jnp.int32(b) for b, _ in pairs]), pick(t, [s for _, s in pairs]), r0, m, n0, nn)

    half = rows // 2
    own_i.wait()
    half_squares(OWN, 0, rows)
    blocks([OWN], [q])
    a_up[0].wait_recv()
    go(f_up[0])
    a_dn[0].wait_recv()
    go(f_dn[0])
    l0r.wait_recv()
    p0r.wait_recv()
    blocks([OWN], [q_sib])
    a_up[1].wait_recv()
    go(f_up[1])
    a_dn[1].wait_recv()
    go(f_dn[1])
    for cp in b_up + b_dn:
        go(cp)
    half_squares(NEAR, 0, rows)
    p1r.wait_recv()
    go(p2)
    l_zr[0].wait_recv()
    go(l_f[0])
    l_zr[1].wait_recv()
    go(l_f[1])
    go(v1)
    go(v2)
    go(v0)
    lh = nl // 2
    blocks([NEAR], [q, q_sib])
    blocks([OWN, NEAR], [q_oth], 0, rows, 0, lh)
    p2r.wait_recv()
    l_fr[0].wait_recv()
    l_fr[1].wait_recv()
    blocks([OWN, NEAR], [q_osib], 0, rows, 0, lh)
    f_up[0].wait_recv()
    f_dn[0].wait_recv()
    half_squares(FAR, 0, half)
    blocks([FAR], [q, q_sib], 0, half)
    l_zr[2].wait_recv()
    go(l_f[2])
    l_zr[3].wait_recv()
    go(l_f[3])
    blocks([OWN, NEAR], [q_oth], 0, rows, lh, lh)
    blocks([FAR], [q_oth], 0, half)
    f_up[1].wait_recv()
    f_dn[1].wait_recv()
    half_squares(FAR, half, half)
    l_fr[2].wait_recv()
    l_fr[3].wait_recv()
    blocks([FAR], [q, q_sib, q_oth, q_osib], half, half)
    blocks([FAR], [q_osib], 0, half)
    blocks([OWN, NEAR], [q_osib], 0, rows, lh, lh)
    b_up[0].wait_recv()
    b_dn[0].wait_recv()
    half_squares(NEXT, 0, half)
    blocks([NEXT], [q, q_sib, q_oth, q_osib], 0, half)
    own_v.wait()
    v1r.wait_recv()
    v2r.wait_recv()
    go(v3)
    b_up[1].wait_recv()
    b_dn[1].wait_recv()
    half_squares(NEXT, half, half)
    blocks([NEXT], [q, q_sib, q_oth, q_osib], half, half)

    def gather(buf, me, others, base, send=True, wait=True):
        for i, (_, d) in enumerate(others if send else []):
            go(pltpu.make_async_remote_copy(
                src_ref=buf.at[me], dst_ref=buf.at[me], send_sem=gs.at[base + i], recv_sem=gr.at[base + me],
                device_id=d, device_id_type=pl.DeviceIdType.MESH))
        for p, d in others if wait else []:
            pltpu.make_async_remote_copy(
                src_ref=buf.at[me], dst_ref=buf.at[p], send_sem=gs.at[base], recv_sem=gr.at[base + p],
                device_id=d, device_id_type=pl.DeviceIdType.MESH).wait_recv()

    for s in range(4):
        ldx[s // 2, mine[(0, 2)[s // 2]], :, pl.ds((s % 2) * nl, nl)] = jnp.sum(colacc[s], axis=0, keepdims=True)
    routes = ((0, 2), (2, 0))
    for i, (one, two) in enumerate(routes):
        gather(ldx.at[i], mine[one], groups[one], 8 * i, wait=False)
    for blk in range(4):
        for k in range(4):
            t = jnp.sum(rowacc[blk, rq(k), :].T, axis=0, keepdims=True)
            row, part = (k // 2, k % 2) if blk == OWN else (k % 2, k // 2)
            degs[blk, row:row + 1, part * qr:(part + 1) * qr] = t
    dsrc = [(NEAR, 0, 0, 0, down), (NEAR, 1, 1, 1, up), (NEXT, 0, 0, 1, down), (NEXT, 1, 1, 0, up),
            (FAR, 0, 2, 0, far), (FAR, 1, 2, 1, far)]
    for i, (one, two) in enumerate(routes):
        gather(ldx.at[i], mine[one], groups[one], 8 * i, send=False)
        tot = ldx[i, 0]
        for k in range(1, GROUP):
            tot = tot + ldx[i, k]
        ldz[i, pos[two]] = tot
        gather(ldz.at[i], pos[two], lines[two], 16 + 4 * i, wait=False)
    dcp = []
    for i, (blk, row, slot, h, d) in enumerate(dsrc):
        dcp.append(rc(28 + i, degs.at[blk, pl.ds(row, 1)], degr.at[slot, pl.ds(h, 1)], d))
        go(dcp[-1])
    for i, (one, two) in enumerate(routes):
        gather(ldz.at[i], pos[two], lines[two], 16 + 4 * i, send=False)
        tot = ldz[i, 0]
        for k in range(1, NZ):
            tot = tot + ldz[i, k]
        rsv[:, pl.ds(i * 2 * nl, 2 * nl)] = lax.rsqrt(tot)

    v0r.wait_recv()
    v3r.wait_recv()

    def product(blk, acc):
        acc[...] = jnp.zeros_like(acc)

        @pl.loop(0, 4)
        def _(s):
            part = None
            for k in range(0, nl, 256):
                for w in range(k, k + 256, 128):
                    off = pl.multiple_of(s * nl + w, 128)
                    rv = jnp.broadcast_to(rsv[:, pl.ds(off, 128)], (RC, 128))
                    for r in range(0, rows, RC):
                        scl[pl.ds(r, RC), pl.ds(w, 128)] = (kmat[blk, s, pl.ds(r, RC), pl.ds(w, 128)] * rv).astype(bf16)
                d = jnp.dot(scl[:, pl.ds(k, 256)], evs[s, pl.ds(k, 256), :], preferred_element_type=f32)
                part = d if part is None else part + d
            acc[...] += part

    def send_half(n, acc, h, d, add=None):
        for k in range(2):
            v = acc[rq(2 * k + h)]
            if add is not None:
                v = v + precv[add, rq(k)].astype(f32)
            psend[n, rq(k)] = v.astype(psend.dtype)
        cp = rc(34 + n, psend.at[n], precv.at[n], d)
        go(cp)
        return cp

    product(FAR, acc)
    r0 = send_half(0, acc, 0, up)
    r1 = send_half(1, acc, 1, down)
    product(NEAR, acc)
    r2 = send_half(2, acc, 0, down)
    r3 = send_half(3, acc, 1, up)
    product(NEXT, acc)
    product(OWN, acc2)
    r0.wait_recv()
    r4 = send_half(4, acc, 1, up, 0)
    r1.wait_recv()
    r5 = send_half(5, acc, 0, down, 1)

    nrows, nlands = float(NROWS), float(LANDMARKS)
    factor = (nrows * nlands) ** 0.5
    for cp in dcp:
        cp.wait_recv()
    r2.wait_recv()
    r3.wait_recv()
    r4.wait_recv()
    r5.wait_recv()
    inv = 1.0 / eigvals[...]
    for h in range(2):
        deg = degs[OWN, h:h + 1, :]
        for k in range(3):
            deg = deg + degr[k, h:h + 1, :]
        f = factor / jnp.sqrt(deg)
        col = jnp.broadcast_to(f, (128, halfr)).T
        for w in range(0, 256, 128):
            v = acc2[pl.ds(h * halfr, halfr), pl.ds(w, 128)] + precv[2 + h, :, pl.ds(w, 128)].astype(f32)
            v = v + precv[4 + h, :, pl.ds(w, 128)].astype(f32)
            coords[pl.ds(h * halfr, halfr), pl.ds(w, 128)] = v * col * inv[:, w:w + 128]

    cv = coords[...]
    top = cv.astype(bf16)
    low = (cv - top.astype(f32)).astype(bf16)
    topt, lowt = top.T, low.T
    for i, (a, b) in enumerate(((0, 0), (0, 128), (128, 128))):
        v = jnp.dot(topt[a:a + 128], top[:, b:b + 128], preferred_element_type=f32)
        v = v + jnp.dot(topt[a:a + 128], low[:, b:b + 128], preferred_element_type=f32)
        v = v + jnp.dot(lowt[a:a + 128], top[:, b:b + 128], preferred_element_type=f32)
        gpart[i] = v.reshape(gpart.shape[1:])
    for i in range(3):
        g = mine[i]
        for j, (p, d) in enumerate(groups[i]):
            go(pltpu.make_async_remote_copy(
                src_ref=gpart.at[i, p], dst_ref=grx.at[i, g], send_sem=gs.at[24 + 8 * i + j], recv_sem=gr.at[24 + 8 * i + g],
                device_id=d, device_id_type=pl.DeviceIdType.MESH))
    for i in range(3):
        two = (i + 1) % 3
        for p, d in groups[i]:
            pltpu.make_async_remote_copy(
                src_ref=gpart.at[i, p], dst_ref=grx.at[i, p], send_sem=gs.at[24 + 8 * i], recv_sem=gr.at[24 + 8 * i + p],
                device_id=d, device_id_type=pl.DeviceIdType.MESH).wait_recv()
        tot = gpart[i, mine[i]]
        for p, _ in groups[i]:
            tot = tot + grx[i, p]
        gry[i, pos[two]] = tot
        gather(gry.at[i], pos[two], lines[two], 48 + 4 * i, wait=False)
    for i in range(3):
        two, three = (i + 1) % 3, (i + 2) % 3
        gather(gry.at[i], pos[two], lines[two], 48 + 4 * i, send=False)
        tot = gry[i, 0]
        for k in range(1, NY):
            tot = tot + gry[i, k]
        grz[i, pos[three]] = tot
        gather(grz.at[i], pos[three], lines[three], 60 + 4 * i, wait=False)
    for i in range(3):
        three = (i + 2) % 3
        gather(grz.at[i], pos[three], lines[three], 60 + 4 * i, send=False)
        tot = grz[i, 0]
        for k in range(1, NZ):
            tot = tot + grz[i, k]
        gfull[i, mine[i]] = tot * (1.0 / NROWS)
        gather(gfull.at[i], mine[i], groups[i], 72 + 8 * i, wait=False)
    for i, (a, b) in enumerate(((0, 0), (0, 128), (128, 128))):
        gather(gfull.at[i], mine[i], groups[i], 72 + 8 * i, send=False)
        v = gfull[i].reshape(128, 128)
        gram[a:a + 128, b:b + 128] = v
        if a != b:
            gram[b:b + 128, a:a + 128] = v.T

    for cp in sends:
        cp.wait_send()
NROWS, LANDMARKS = 65536, 16384


def per_device(items, landmarks, scales, eigvecs, eigvals):
    rows, dim = items.shape
    nl, width = eigvecs.shape
    half = rows // 2
    anyspec = pl.BlockSpec(memory_space=pl.ANY)
    vspec = pl.BlockSpec(memory_space=pltpu.VMEM)
    V, DMA = pltpu.VMEM, pltpu.SemaphoreType.DMA
    return pl.pallas_call(
        kernel,
        out_shape=(jax.ShapeDtypeStruct((rows, width), f32), jax.ShapeDtypeStruct((width, width), f32)),
        in_specs=[anyspec, anyspec, anyspec, vspec, vspec],
        out_specs=(vspec, vspec),
        scratch_shapes=[
            V((4, rows, dim), bf16), V((4, nl, dim), bf16), V((4, nl, width), bf16), V((4, 8, nl), f32),
            V((4, rows, 128), f32), V((4, 4, rows, nl), f32), V((4, rows, 128), f32), V((4, 8, nl), f32),
            V((2, rows, NTILE), f32),
            V((2, GROUP, 1, 2 * nl), f32), V((2, NZ, 1, 2 * nl), f32), V((1, 4 * nl), f32), V((4, 2, half), f32), V((3, 2, half), f32),
            V((rows, nl), bf16), V((rows, width), f32), V((rows, width), f32), V((6, half, width), PT), V((6, half, width), PT),
            V((3, GROUP, 16, 128), f32), V((3, GROUP, 16, 128), f32), V((3, NY, 16, 128), f32), V((3, NZ, 16, 128), f32),
            V((3, GROUP, 16, 128), f32),
            DMA((3,)), DMA((40,)), DMA((40,)), DMA((96,)), DMA((96,)),
        ],
        compiler_params=pltpu.CompilerParams(collective_id=0, has_side_effects=True, vmem_limit_bytes=62 * 2**20),
    )(items, landmarks, eigvecs, scales.reshape(1, nl), eigvals.reshape(1, width))


def solution(mesh):
    return jax.shard_map(
        per_device, mesh=mesh,
        in_specs=(P(("dp", "land"), None), P("land", None), P("land"), P("land", None), P()),
        out_specs=(P(("dp", "land"), None), P()), check_vma=False)
```

```python
import jax
import jax.numpy as jnp
from jax import lax
from jax.experimental import pallas as pl
from jax.experimental.pallas import tpu as pltpu
from jax.sharding import PartitionSpec as P


f32, bf16 = jnp.float32, jnp.bfloat16
LOG2E = 1.4426950408889634
PT = jnp.bfloat16
NTILE = 512
OWN, NEAR, NEXT, FAR = 0, 1, 2, 3
NX = NY = NZ = 4
GROUP = 8


def place(x, y, z, c):
    return {"dp": lax.div(z, 2) * NX + x, "land": lax.rem(z, 2) * 8 + y * 2 + c}


def kernel(items, lands, vecs, scales, eigvals, coords_out, gram_out, coords, gram,
           it, lmk, evs, lp, rh, kmat, rowacc, colacc, cross,
           ldx, ldz, rsv, degs, degr, scl, acc, acc2, psend, precv,
           gpart, grx, gry, grz, gfull,
           loc, ssem, rsem, gs, gr):
    rows, halfr = items.shape[0], items.shape[0] // 2
    nl = lands.shape[0]
    halfl = nl // 2
    dp, land = lax.axis_index("dp"), lax.axis_index("land")
    x, zh = lax.rem(dp, NX), lax.div(dp, NX)
    c, y, zl = lax.rem(land, 2), lax.rem(lax.div(land, 2), NY), lax.div(land, 8)
    z = zh * 2 + zl
    yn, yp = lax.rem(y + 1, NY), lax.rem(y + NY - 1, NY)
    zn, zp = lax.rem(z + 1, NZ), lax.rem(z + NZ - 1, NZ)
    yfar = lax.rem(y + 2, NY)
    up, down, far = place(x, yn, z, c), place(x, yp, z, c), place(x, yfar, z, c)
    zup, zdown = place(x, y, zn, c), place(x, y, zp, c)
    sib = place(x, y, z, 1 - c)
    pos = (x, y, z)

    def at(axis, v, core):
        v = [v if k == axis else pos[k] for k in range(3)]
        return place(*v, core)

    groups, lines, mine = [], [], []
    for axis in range(3):
        g = pos[axis] * 2 + c
        mine.append(g)
        groups.append([])
        for k in range(1, GROUP):
            p = lax.rem(g + k, GROUP)
            groups[axis].append((p, at(axis, lax.div(p, 2), lax.rem(p, 2))))
        lines.append([])
        for k in range(1, NX):
            p = lax.rem(pos[axis] + k, NX)
            lines[axis].append((p, at(axis, p, c)))
    q = zl * 2 + c
    q_sib, q_oth, q_osib = zl * 2 + 1 - c, (1 - zl) * 2 + c, (1 - zl) * 2 + 1 - c

    barrier = pltpu.get_barrier_semaphore()
    peers = [sib] + [at(axis, lax.rem(pos[axis] + k, NX), core) for axis in range(3) for k in range(1, NX) for core in (c, 1 - c)]
    for d in peers:
        pl.semaphore_signal(barrier, inc=1, device_id=d, device_id_type=pl.DeviceIdType.MESH)

    own_i = pltpu.make_async_copy(items, it.at[OWN], loc.at[0])
    own_l = pltpu.make_async_copy(lands, lmk.at[q], loc.at[1])
    own_v = pltpu.make_async_copy(vecs, evs.at[q], loc.at[2])
    own_l.start()
    own_i.start()
    own_v.start()

    sends = []

    def rc(i, src, dst, d):
        return pltpu.make_async_remote_copy(
            src_ref=src, dst_ref=dst, send_sem=ssem.at[i], recv_sem=rsem.at[i],
            device_id=d, device_id_type=pl.DeviceIdType.MESH)

    def go(cp):
        cp.start()
        sends.append(cp)

    qr, ql = rows // 4, nl // 4

    def rq(k, n=1):
        return pl.ds(k * qr, n * qr)

    def lq(k):
        return pl.ds(k * ql, ql)

    a_up = [rc(k, items.at[rq(k)], it.at[NEAR, rq(2 * k)], up) for k in range(2)]
    a_dn = [rc(2 + k, items.at[rq(2 + k)], it.at[NEAR, rq(2 * k + 1)], down) for k in range(2)]
    f_up = [rc(4 + k, it.at[NEAR, rq(2 * k)], it.at[FAR, rq(2 * k)], up) for k in range(2)]
    f_dn = [rc(6 + k, it.at[NEAR, rq(2 * k + 1)], it.at[FAR, rq(2 * k + 1)], down) for k in range(2)]
    b_up = [rc(8 + k, items.at[rq(2 + k)], it.at[NEXT, rq(2 * k)], up) for k in range(2)]
    b_dn = [rc(10 + k, items.at[rq(k)], it.at[NEXT, rq(2 * k + 1)], down) for k in range(2)]
    zdev = [zup, zdown, zup, zdown]
    l_z = [rc(12 + k, lands.at[lq(k)], lmk.at[q, lq(k)], zdev[k]) for k in range(4)]
    l_zr = [rc(12 + k, lands.at[lq(k)], lmk.at[q_oth, lq(k)], zdev[k]) for k in range(4)]
    l_f = [rc(16 + k, lmk.at[q_oth, lq(k)], lmk.at[q_oth, lq(k)], sib) for k in range(4)]
    l_fr = [rc(16 + k, lmk.at[q_oth, lq(k)], lmk.at[q_osib, lq(k)], sib) for k in range(4)]
    l0 = rc(20, lands, lmk.at[q], sib)
    l0r = rc(20, lands, lmk.at[q_sib], sib)
    p0 = rc(21, lp.at[q], lp.at[q], sib)
    p0r = rc(21, lp.at[q], lp.at[q_sib], sib)
    p1 = rc(22, lp.at[q], lp.at[q], zup)
    p1r = rc(22, lp.at[q], lp.at[q_oth], zup)
    p2 = rc(23, lp.at[q_oth], lp.at[q_oth], sib)
    p2r = rc(23, lp.at[q_oth], lp.at[q_osib], sib)
    llo, lhi = pl.ds(0, halfl), pl.ds(halfl, halfl)
    v0 = rc(24, vecs, evs.at[q], sib)
    v0r = rc(24, vecs, evs.at[q_sib], sib)
    v1 = rc(25, vecs.at[llo], evs.at[q, llo], zup)
    v1r = rc(25, vecs.at[llo], evs.at[q_oth, llo], zup)
    v2 = rc(26, vecs.at[lhi], evs.at[q, lhi], zdown)
    v2r = rc(26, vecs.at[lhi], evs.at[q_oth, lhi], zdown)
    v3 = rc(27, evs.at[q_oth], evs.at[q_oth], sib)
    v3r = rc(27, evs.at[q_oth], evs.at[q_osib], sib)

    own_l.wait()
    for r in range(0, nl, 128):
        part = None
        for k in range(0, lands.shape[1], 128):
            v = lmk[q, pl.ds(r, 128), pl.ds(k, 128)].astype(f32)
            part = v * v if part is None else part + v * v
        sq = jnp.sum(part.T, axis=0, keepdims=True)
        s = scales[:, pl.ds(r, 128)] * LOG2E
        lp[q, 0:1, pl.ds(r, 128)] = s + s
        lp[q, 1:2, pl.ds(r, 128)] = -s * sq
        lp[q, 2:8, pl.ds(r, 128)] = jnp.zeros((6, 128), f32)

    pl.semaphore_wait(barrier, len(peers))
    for cp in a_up + a_dn:
        go(cp)
    go(p1)
    go(l0)
    go(p0)
    for cp in l_z:
        go(cp)

    colacc[...] = jnp.zeros_like(colacc)
    rowacc[...] = jnp.zeros_like(rowacc)

    def half_squares(blk, r0, n):
        for r in range(r0, r0 + n, 128):
            part = None
            for k in range(0, items.shape[1], 128):
                v = it[blk, pl.ds(r, 128), pl.ds(k, 128)].astype(f32)
                part = v * v if part is None else part + v * v
            rh[blk, pl.ds(r, 128), :] = jnp.broadcast_to(0.5 * jnp.sum(part, axis=1, keepdims=True), (128, 128))

    NT, RC = NTILE, 64

    def block(blk, slot, r0, m, n0, nn):
        for n in range(n0, n0 + nn, NT):
            buf = (n // NT) % 2
            cross[buf, pl.ds(0, m)] = lax.dot_general(
                it[blk, pl.ds(r0, m), :], lmk[slot, pl.ds(n, NT), :], (((1,), (1,)), ((), ())), preferred_element_type=f32)
            col = [None] * (NT // 128)
            for r in range(0, m, RC):
                half_sq = rh[blk, pl.ds(r0 + r, RC), :]
                row = None
                for w in range(NT // 128):
                    cols = pl.ds(n + w * 128, 128)
                    t = (cross[buf, pl.ds(r, RC), pl.ds(w * 128, 128)] - half_sq) * lp[slot, 0:1, cols] + lp[slot, 1:2, cols]
                    kv = jnp.exp2(t)
                    kmat[blk, slot, pl.ds(r0 + r, RC), cols] = kv
                    row = kv if row is None else row + kv
                    ks = jnp.sum(kv.reshape(RC // 8, 8, 128), axis=0)
                    col[w] = ks if col[w] is None else col[w] + ks
                rowacc[blk, pl.ds(r0 + r, RC), :] += row
            for w in range(NT // 128):
                colacc[slot, :, pl.ds(n + w * 128, 128)] += col[w]

    def blocks(blks, slots, r0=0, m=rows, n0=0, nn=nl):
        pairs = [(b, s) for b in blks for s in slots]
        n = len(pairs)

        def pick(t, values):
            out = values[-1]
            for i in range(n - 2, -1, -1):
                out = jnp.where(t == i, values[i], out)
            return out

        @pl.loop(0, n)
        def _(t):
            block(pick(t, [jnp.int32(b) for b, _ in pairs]), pick(t, [s for _, s in pairs]), r0, m, n0, nn)

    half = rows // 2
    own_i.wait()
    half_squares(OWN, 0, rows)
    blocks([OWN], [q])
    a_up[0].wait_recv()
    go(f_up[0])
    a_dn[0].wait_recv()
    go(f_dn[0])
    l0r.wait_recv()
    p0r.wait_recv()
    blocks([OWN], [q_sib])
    a_up[1].wait_recv()
    go(f_up[1])
    a_dn[1].wait_recv()
    go(f_dn[1])
    for cp in b_up + b_dn:
        go(cp)
    half_squares(NEAR, 0, rows)
    p1r.wait_recv()
    go(p2)
    l_zr[0].wait_recv()
    go(l_f[0])
    l_zr[1].wait_recv()
    go(l_f[1])
    go(v1)
    go(v2)
    go(v0)
    lh = nl // 2
    blocks([NEAR], [q, q_sib])
    blocks([OWN, NEAR], [q_oth], 0, rows, 0, lh)
    p2r.wait_recv()
    l_fr[0].wait_recv()
    l_fr[1].wait_recv()
    blocks([OWN, NEAR], [q_osib], 0, rows, 0, lh)
    f_up[0].wait_recv()
    f_dn[0].wait_recv()
    half_squares(FAR, 0, half)
    blocks([FAR], [q, q_sib], 0, half)
    blocks([FAR], [q_oth, q_osib], 0, half, 0, lh)
    l_zr[2].wait_recv()
    go(l_f[2])
    l_zr[3].wait_recv()
    go(l_f[3])
    blocks([OWN, NEAR], [q_oth], 0, rows, lh, lh)
    blocks([FAR], [q_oth], 0, half, lh, lh)
    f_up[1].wait_recv()
    f_dn[1].wait_recv()
    half_squares(FAR, half, half)
    l_fr[2].wait_recv()
    l_fr[3].wait_recv()
    blocks([FAR], [q, q_sib, q_oth, q_osib], half, half)
    blocks([FAR], [q_osib], 0, half, lh, lh)
    blocks([OWN, NEAR], [q_osib], 0, rows, lh, lh)
    b_up[0].wait_recv()
    b_dn[0].wait_recv()
    half_squares(NEXT, 0, half)
    blocks([NEXT], [q, q_sib, q_oth, q_osib], 0, half)
    own_v.wait()
    v1r.wait_recv()
    v2r.wait_recv()
    go(v3)
    b_up[1].wait_recv()
    b_dn[1].wait_recv()
    half_squares(NEXT, half, half)
    blocks([NEXT], [q, q_sib, q_oth, q_osib], half, half)

    def gather(buf, me, others, base, send=True, wait=True):
        for i, (_, d) in enumerate(others if send else []):
            go(pltpu.make_async_remote_copy(
                src_ref=buf.at[me], dst_ref=buf.at[me], send_sem=gs.at[base + i], recv_sem=gr.at[base + me],
                device_id=d, device_id_type=pl.DeviceIdType.MESH))
        for p, d in others if wait else []:
            pltpu.make_async_remote_copy(
                src_ref=buf.at[me], dst_ref=buf.at[p], send_sem=gs.at[base], recv_sem=gr.at[base + p],
                device_id=d, device_id_type=pl.DeviceIdType.MESH).wait_recv()

    for s in range(4):
        ldx[s // 2, mine[(0, 2)[s // 2]], :, pl.ds((s % 2) * nl, nl)] = jnp.sum(colacc[s], axis=0, keepdims=True)
    routes = ((0, 2), (2, 0))
    for i, (one, two) in enumerate(routes):
        gather(ldx.at[i], mine[one], groups[one], 8 * i, wait=False)
    for blk in range(4):
        for k in range(4):
            t = jnp.sum(rowacc[blk, rq(k), :].T, axis=0, keepdims=True)
            row, part = (k // 2, k % 2) if blk == OWN else (k % 2, k // 2)
            degs[blk, row:row + 1, part * qr:(part + 1) * qr] = t
    dsrc = [(NEAR, 0, 0, 0, down), (NEAR, 1, 1, 1, up), (NEXT, 0, 0, 1, down), (NEXT, 1, 1, 0, up),
            (FAR, 0, 2, 0, far), (FAR, 1, 2, 1, far)]
    for i, (one, two) in enumerate(routes):
        gather(ldx.at[i], mine[one], groups[one], 8 * i, send=False)
        tot = ldx[i, 0]
        for k in range(1, GROUP):
            tot = tot + ldx[i, k]
        ldz[i, pos[two]] = tot
        gather(ldz.at[i], pos[two], lines[two], 16 + 4 * i, wait=False)
    dcp = []
    for i, (blk, row, slot, h, d) in enumerate(dsrc):
        dcp.append(rc(28 + i, degs.at[blk, pl.ds(row, 1)], degr.at[slot, pl.ds(h, 1)], d))
        go(dcp[-1])
    for i, (one, two) in enumerate(routes):
        gather(ldz.at[i], pos[two], lines[two], 16 + 4 * i, send=False)
        tot = ldz[i, 0]
        for k in range(1, NZ):
            tot = tot + ldz[i, k]
        rsv[:, pl.ds(i * 2 * nl, 2 * nl)] = lax.rsqrt(tot)

    v0r.wait_recv()
    v3r.wait_recv()

    def product(blk, acc, r0=0, m=rows):
        acc[pl.ds(r0, m)] = jnp.zeros((m, acc.shape[1]), f32)

        @pl.loop(0, 4)
        def _(s):
            part = None
            for k in range(0, nl, 256):
                for w in range(k, k + 256, 128):
                    off = pl.multiple_of(s * nl + w, 128)
                    rv = jnp.broadcast_to(rsv[:, pl.ds(off, 128)], (RC, 128))
                    for r in range(r0, r0 + m, RC):
                        scl[pl.ds(r, RC), pl.ds(w, 128)] = (kmat[blk, s, pl.ds(r, RC), pl.ds(w, 128)] * rv).astype(bf16)
                d = jnp.dot(scl[pl.ds(r0, m), pl.ds(k, 256)], evs[s, pl.ds(k, 256), :], preferred_element_type=f32)
                part = d if part is None else part + d
            acc[pl.ds(r0, m)] += part

    def send_part(n, h, d, k, add=None):
        v = acc[rq(2 * k + h)]
        if add is not None:
            v = v + precv[add, rq(k)].astype(f32)
        psend[n, rq(k)] = v.astype(psend.dtype)
        cp = rc(34 + 2 * n + k, psend.at[n, rq(k)], precv.at[n, rq(k)], d)
        go(cp)
        return cp

    first = []
    for k in range(2):
        product(FAR, acc, k * half, half)
        first.append((send_part(0, 0, up, k), send_part(1, 1, down, k)))
    product(NEAR, acc)
    last = []
    for k in range(2):
        last += [send_part(2, 0, down, k), send_part(3, 1, up, k)]
    product(NEXT, acc)
    product(OWN, acc2)
    for k in range(2):
        first[k][0].wait_recv()
        last.append(send_part(4, 1, up, k, 0))
        first[k][1].wait_recv()
        last.append(send_part(5, 0, down, k, 1))

    nrows, nlands = float(NROWS), float(LANDMARKS)
    factor = (nrows * nlands) ** 0.5
    for cp in dcp:
        cp.wait_recv()
    for cp in last:
        cp.wait_recv()
    inv = 1.0 / eigvals[...]
    for h in range(2):
        deg = degs[OWN, h:h + 1, :]
        for k in range(3):
            deg = deg + degr[k, h:h + 1, :]
        f = factor / jnp.sqrt(deg)
        col = jnp.broadcast_to(f, (128, halfr)).T
        for w in range(0, 256, 128):
            v = acc2[pl.ds(h * halfr, halfr), pl.ds(w, 128)] + precv[2 + h, :, pl.ds(w, 128)].astype(f32)
            v = v + precv[4 + h, :, pl.ds(w, 128)].astype(f32)
            coords[pl.ds(h * halfr, halfr), pl.ds(w, 128)] = v * col * inv[:, w:w + 128]

    out_c = pltpu.make_async_copy(coords, coords_out, loc.at[3])
    out_c.start()

    cv = coords[...]
    top = cv.astype(bf16)
    low = (cv - top.astype(f32)).astype(bf16)
    topt, lowt = top.T, low.T
    for i, (a, b) in enumerate(((0, 0), (0, 128), (128, 128))):
        v = jnp.dot(topt[a:a + 128], top[:, b:b + 128], preferred_element_type=f32)
        v = v + jnp.dot(topt[a:a + 128], low[:, b:b + 128], preferred_element_type=f32)
        v = v + jnp.dot(lowt[a:a + 128], top[:, b:b + 128], preferred_element_type=f32)
        gpart[i] = v.reshape(gpart.shape[1:])
    for i in range(3):
        g = mine[i]
        for j, (p, d) in enumerate(groups[i]):
            go(pltpu.make_async_remote_copy(
                src_ref=gpart.at[i, p], dst_ref=grx.at[i, g], send_sem=gs.at[24 + 8 * i + j], recv_sem=gr.at[24 + 8 * i + g],
                device_id=d, device_id_type=pl.DeviceIdType.MESH))
    for i in range(3):
        two = (i + 1) % 3
        for p, d in groups[i]:
            pltpu.make_async_remote_copy(
                src_ref=gpart.at[i, p], dst_ref=grx.at[i, p], send_sem=gs.at[24 + 8 * i], recv_sem=gr.at[24 + 8 * i + p],
                device_id=d, device_id_type=pl.DeviceIdType.MESH).wait_recv()
        tot = gpart[i, mine[i]]
        for p, _ in groups[i]:
            tot = tot + grx[i, p]
        gry[i, pos[two]] = tot
        gather(gry.at[i], pos[two], lines[two], 48 + 4 * i, wait=False)
    for i in range(3):
        two, three = (i + 1) % 3, (i + 2) % 3
        gather(gry.at[i], pos[two], lines[two], 48 + 4 * i, send=False)
        tot = gry[i, 0]
        for k in range(1, NY):
            tot = tot + gry[i, k]
        grz[i, pos[three]] = tot
        gather(grz.at[i], pos[three], lines[three], 60 + 4 * i, wait=False)
    for i in range(3):
        three = (i + 2) % 3
        gather(grz.at[i], pos[three], lines[three], 60 + 4 * i, send=False)
        tot = grz[i, 0]
        for k in range(1, NZ):
            tot = tot + grz[i, k]
        gfull[i, mine[i]] = tot * (1.0 / NROWS)
        gather(gfull.at[i], mine[i], groups[i], 72 + 8 * i, wait=False)
    for i, (a, b) in enumerate(((0, 0), (0, 128), (128, 128))):
        gather(gfull.at[i], mine[i], groups[i], 72 + 8 * i, send=False)
        v = gfull[i].reshape(128, 128)
        gram[a:a + 128, b:b + 128] = v
        if a != b:
            gram[b:b + 128, a:a + 128] = v.T

    out_g = pltpu.make_async_copy(gram, gram_out, loc.at[4])
    out_g.start()
    for cp in sends:
        cp.wait_send()
    out_c.wait()
    out_g.wait()

def copy_out(c, g, c_out, g_out, sem):
    n = c.shape[0] // 4
    cps = [pltpu.make_async_copy(c.at[pl.ds(k * n, n)], c_out.at[pl.ds(k * n, n)], sem.at[k]) for k in range(4)]
    n = g.shape[0] // 2
    cps += [pltpu.make_async_copy(g.at[pl.ds(k * n, n)], g_out.at[pl.ds(k * n, n)], sem.at[4 + k]) for k in range(2)]
    for cp in cps:
        cp.start()
    for cp in cps:
        cp.wait()


NROWS, LANDMARKS = 65536, 16384


def per_device(items, landmarks, scales, eigvecs, eigvals):
    rows, dim = items.shape
    nl, width = eigvecs.shape
    half = rows // 2
    anyspec = pl.BlockSpec(memory_space=pl.ANY)
    vspec = pl.BlockSpec(memory_space=pltpu.VMEM)
    V, DMA = pltpu.VMEM, pltpu.SemaphoreType.DMA
    shapes = (jax.ShapeDtypeStruct((rows, width), f32), jax.ShapeDtypeStruct((width, width), f32))
    results = pl.pallas_call(
        kernel,
        out_shape=shapes,
        in_specs=[anyspec, anyspec, anyspec, vspec, vspec],
        out_specs=(anyspec, anyspec),
        scratch_shapes=[
            V((rows, width), f32), V((width, width), f32),
            V((4, rows, dim), bf16), V((4, nl, dim), bf16), V((4, nl, width), bf16), V((4, 8, nl), f32),
            V((4, rows, 128), f32), V((4, 4, rows, nl), f32), V((4, rows, 128), f32), V((4, 8, nl), f32),
            V((2, rows, NTILE), f32),
            V((2, GROUP, 1, 2 * nl), f32), V((2, NZ, 1, 2 * nl), f32), V((1, 4 * nl), f32), V((4, 2, half), f32), V((3, 2, half), f32),
            V((rows, nl), bf16), V((rows, width), f32), V((rows, width), f32), V((6, half, width), PT), V((6, half, width), PT),
            V((3, GROUP, 16, 128), f32), V((3, GROUP, 16, 128), f32), V((3, NY, 16, 128), f32), V((3, NZ, 16, 128), f32),
            V((3, GROUP, 16, 128), f32),
            DMA((5,)), DMA((46,)), DMA((46,)), DMA((96,)), DMA((96,)),
        ],
        compiler_params=pltpu.CompilerParams(collective_id=0, has_side_effects=True, vmem_limit_bytes=62 * 2**20),
    )(items, landmarks, eigvecs, scales.reshape(1, nl), eigvals.reshape(1, width))
    return pl.pallas_call(
        copy_out, out_shape=shapes, in_specs=[anyspec, anyspec], out_specs=(anyspec, anyspec),
        scratch_shapes=[DMA((6,))])(*results)


def solution(mesh):
    return jax.shard_map(
        per_device, mesh=mesh,
        in_specs=(P(("dp", "land"), None), P("land", None), P("land"), P("land", None), P()),
        out_specs=(P(("dp", "land"), None), P()), check_vma=False)
```

```python
import jax
import jax.numpy as jnp
from jax import lax
from jax.experimental import pallas as pl
from jax.experimental.pallas import tpu as pltpu
from jax.sharding import PartitionSpec as P


f32, bf16 = jnp.float32, jnp.bfloat16
LOG2E = 1.4426950408889634
PT = jnp.bfloat16
NTILE = 512
OWN, NEAR, NEXT, FAR = 0, 1, 2, 3
NX = NY = NZ = 4
GROUP = 8


def place(x, y, z, c):
    return {"dp": lax.div(z, 2) * NX + x, "land": lax.rem(z, 2) * 8 + y * 2 + c}


def kernel(items, lands, vecs, scales, eigvals, coords_out, gram_out, coords, gram,
           it, lmk, evs, lp, rh, kmat, rowacc, colacc, cross,
           ldx, ldz, rsv, degs, degr, scl, acc, acc2, psend, precv,
           gpart, grx, gry, grz, gfull,
           loc, ssem, rsem, gs, gr):
    rows, halfr = items.shape[0], items.shape[0] // 2
    nl = lands.shape[0]
    halfl = nl // 2
    dp, land = lax.axis_index("dp"), lax.axis_index("land")
    x, zh = lax.rem(dp, NX), lax.div(dp, NX)
    c, y, zl = lax.rem(land, 2), lax.rem(lax.div(land, 2), NY), lax.div(land, 8)
    z = zh * 2 + zl
    yn, yp = lax.rem(y + 1, NY), lax.rem(y + NY - 1, NY)
    zn, zp = lax.rem(z + 1, NZ), lax.rem(z + NZ - 1, NZ)
    yfar = lax.rem(y + 2, NY)
    up, down, far = place(x, yn, z, c), place(x, yp, z, c), place(x, yfar, z, c)
    zup, zdown = place(x, y, zn, c), place(x, y, zp, c)
    sib = place(x, y, z, 1 - c)
    pos = (x, y, z)

    def at(axis, v, core):
        v = [v if k == axis else pos[k] for k in range(3)]
        return place(*v, core)

    groups, lines, mine = [], [], []
    for axis in range(3):
        g = pos[axis] * 2 + c
        mine.append(g)
        groups.append([])
        for k in range(1, GROUP):
            p = lax.rem(g + k, GROUP)
            groups[axis].append((p, at(axis, lax.div(p, 2), lax.rem(p, 2))))
        lines.append([])
        for k in range(1, NX):
            p = lax.rem(pos[axis] + k, NX)
            lines[axis].append((p, at(axis, p, c)))
    q = zl * 2 + c
    q_sib, q_oth, q_osib = zl * 2 + 1 - c, (1 - zl) * 2 + c, (1 - zl) * 2 + 1 - c

    barrier = pltpu.get_barrier_semaphore()
    peers = [sib] + [at(axis, lax.rem(pos[axis] + k, NX), core) for axis in range(3) for k in range(1, NX) for core in (c, 1 - c)]
    for d in peers:
        pl.semaphore_signal(barrier, inc=1, device_id=d, device_id_type=pl.DeviceIdType.MESH)

    own_i = pltpu.make_async_copy(items, it.at[OWN], loc.at[0])
    own_l = pltpu.make_async_copy(lands, lmk.at[q], loc.at[1])
    own_v = pltpu.make_async_copy(vecs, evs.at[q], loc.at[2])
    own_l.start()
    own_i.start()
    own_v.start()

    sends = []

    def rc(i, src, dst, d):
        return pltpu.make_async_remote_copy(
            src_ref=src, dst_ref=dst, send_sem=ssem.at[i], recv_sem=rsem.at[i],
            device_id=d, device_id_type=pl.DeviceIdType.MESH)

    def go(cp):
        cp.start()
        sends.append(cp)

    qr, ql = rows // 4, nl // 4

    def rq(k, n=1):
        return pl.ds(k * qr, n * qr)

    def lq(k):
        return pl.ds(k * ql, ql)

    a_up = [rc(k, items.at[rq(k)], it.at[NEAR, rq(2 * k)], up) for k in range(2)]
    a_dn = [rc(2 + k, items.at[rq(2 + k)], it.at[NEAR, rq(2 * k + 1)], down) for k in range(2)]
    f_up = [rc(4 + k, it.at[NEAR, rq(2 * k)], it.at[FAR, rq(2 * k)], up) for k in range(2)]
    f_dn = [rc(6 + k, it.at[NEAR, rq(2 * k + 1)], it.at[FAR, rq(2 * k + 1)], down) for k in range(2)]
    b_up = [rc(8 + k, items.at[rq(2 + k)], it.at[NEXT, rq(2 * k)], up) for k in range(2)]
    b_dn = [rc(10 + k, items.at[rq(k)], it.at[NEXT, rq(2 * k + 1)], down) for k in range(2)]
    zdev = [zup, zdown, zup, zdown]
    l_z = [rc(12 + k, lands.at[lq(k)], lmk.at[q, lq(k)], zdev[k]) for k in range(4)]
    l_zr = [rc(12 + k, lands.at[lq(k)], lmk.at[q_oth, lq(k)], zdev[k]) for k in range(4)]
    l_f = [rc(16 + k, lmk.at[q_oth, lq(k)], lmk.at[q_oth, lq(k)], sib) for k in range(4)]
    l_fr = [rc(16 + k, lmk.at[q_oth, lq(k)], lmk.at[q_osib, lq(k)], sib) for k in range(4)]
    l0 = rc(20, lands, lmk.at[q], sib)
    l0r = rc(20, lands, lmk.at[q_sib], sib)
    p0 = rc(21, lp.at[q], lp.at[q], sib)
    p0r = rc(21, lp.at[q], lp.at[q_sib], sib)
    p1 = rc(22, lp.at[q], lp.at[q], zup)
    p1r = rc(22, lp.at[q], lp.at[q_oth], zup)
    p2 = rc(23, lp.at[q_oth], lp.at[q_oth], sib)
    p2r = rc(23, lp.at[q_oth], lp.at[q_osib], sib)
    llo, lhi = pl.ds(0, halfl), pl.ds(halfl, halfl)
    v0 = rc(24, vecs, evs.at[q], sib)
    v0r = rc(24, vecs, evs.at[q_sib], sib)
    v1 = rc(25, vecs.at[llo], evs.at[q, llo], zup)
    v1r = rc(25, vecs.at[llo], evs.at[q_oth, llo], zup)
    v2 = rc(26, vecs.at[lhi], evs.at[q, lhi], zdown)
    v2r = rc(26, vecs.at[lhi], evs.at[q_oth, lhi], zdown)
    v3 = rc(27, evs.at[q_oth], evs.at[q_oth], sib)
    v3r = rc(27, evs.at[q_oth], evs.at[q_osib], sib)

    own_l.wait()
    for r in range(0, nl, 128):
        part = None
        for k in range(0, lands.shape[1], 128):
            v = lmk[q, pl.ds(r, 128), pl.ds(k, 128)].astype(f32)
            part = v * v if part is None else part + v * v
        sq = jnp.sum(part.T, axis=0, keepdims=True)
        s = scales[:, pl.ds(r, 128)] * LOG2E
        lp[q, 0:1, pl.ds(r, 128)] = s + s
        lp[q, 1:2, pl.ds(r, 128)] = -s * sq
        lp[q, 2:8, pl.ds(r, 128)] = jnp.zeros((6, 128), f32)

    pl.semaphore_wait(barrier, len(peers))
    for cp in a_up + a_dn:
        go(cp)
    go(p1)
    go(l0)
    go(p0)
    for cp in l_z:
        go(cp)

    colacc[...] = jnp.zeros_like(colacc)
    rowacc[...] = jnp.zeros_like(rowacc)

    def half_squares(blk, r0, n):
        for r in range(r0, r0 + n, 128):
            part = None
            for k in range(0, items.shape[1], 128):
                v = it[blk, pl.ds(r, 128), pl.ds(k, 128)].astype(f32)
                part = v * v if part is None else part + v * v
            rh[blk, pl.ds(r, 128), :] = jnp.broadcast_to(0.5 * jnp.sum(part, axis=1, keepdims=True), (128, 128))

    NT, RC = NTILE, 64

    def block(blk, slot, r0, m, n0, nn):
        for n in range(n0, n0 + nn, NT):
            buf = (n // NT) % 2
            cross[buf, pl.ds(0, m)] = lax.dot_general(
                it[blk, pl.ds(r0, m), :], lmk[slot, pl.ds(n, NT), :], (((1,), (1,)), ((), ())), preferred_element_type=f32)
            col = [None] * (NT // 128)
            for r in range(0, m, RC):
                half_sq = rh[blk, pl.ds(r0 + r, RC), :]
                row = None
                for w in range(NT // 128):
                    cols = pl.ds(n + w * 128, 128)
                    t = (cross[buf, pl.ds(r, RC), pl.ds(w * 128, 128)] - half_sq) * lp[slot, 0:1, cols] + lp[slot, 1:2, cols]
                    kv = jnp.exp2(t)
                    kmat[blk, slot, pl.ds(r0 + r, RC), cols] = kv
                    row = kv if row is None else row + kv
                    ks = jnp.sum(kv.reshape(RC // 8, 8, 128), axis=0)
                    col[w] = ks if col[w] is None else col[w] + ks
                rowacc[blk, pl.ds(r0 + r, RC), :] += row
            for w in range(NT // 128):
                colacc[slot, :, pl.ds(n + w * 128, 128)] += col[w]

    def blocks(blks, slots, r0=0, m=rows, n0=0, nn=nl, step=1):
        pairs = [(b, s) for b in blks for s in slots]
        n = len(pairs)

        def pick(t, values):
            out = values[-1]
            for i in range(n - 2, -1, -1):
                out = jnp.where(t == i, values[i], out)
            return out

        @pl.loop(0, n // step)
        def _(t0):
            for u in range(step):
                t = t0 * step + u
                block(pick(t, [jnp.int32(b) for b, _ in pairs]), pick(t, [s for _, s in pairs]), r0, m, n0, nn)

    half = rows // 2
    own_i.wait()
    half_squares(OWN, 0, rows)
    blocks([OWN], [q])
    a_up[0].wait_recv()
    go(f_up[0])
    a_dn[0].wait_recv()
    go(f_dn[0])
    l0r.wait_recv()
    p0r.wait_recv()
    blocks([OWN], [q_sib])
    a_up[1].wait_recv()
    go(f_up[1])
    a_dn[1].wait_recv()
    go(f_dn[1])
    for cp in b_up + b_dn:
        go(cp)
    half_squares(NEAR, 0, rows)
    p1r.wait_recv()
    go(p2)
    l_zr[0].wait_recv()
    go(l_f[0])
    l_zr[1].wait_recv()
    go(l_f[1])
    go(v1)
    go(v2)
    go(v0)
    lh = nl // 2
    blocks([NEAR], [q, q_sib], step=2)
    blocks([OWN, NEAR], [q_oth], 0, rows, 0, lh)
    p2r.wait_recv()
    l_fr[0].wait_recv()
    l_fr[1].wait_recv()
    blocks([OWN, NEAR], [q_osib], 0, rows, 0, lh)
    f_up[0].wait_recv()
    f_dn[0].wait_recv()
    half_squares(FAR, 0, half)
    blocks([FAR], [q, q_sib], 0, half)
    blocks([FAR], [q_oth, q_osib], 0, half, 0, lh)
    l_zr[2].wait_recv()
    go(l_f[2])
    l_zr[3].wait_recv()
    go(l_f[3])
    blocks([OWN, NEAR], [q_oth], 0, rows, lh, lh, step=2)
    blocks([FAR], [q_oth], 0, half, lh, lh)
    f_up[1].wait_recv()
    f_dn[1].wait_recv()
    half_squares(FAR, half, half)
    l_fr[2].wait_recv()
    l_fr[3].wait_recv()
    blocks([FAR], [q, q_sib, q_oth, q_osib], half, half, step=4)
    blocks([FAR], [q_osib], 0, half, lh, lh)
    blocks([OWN, NEAR], [q_osib], 0, rows, lh, lh, step=2)
    b_up[0].wait_recv()
    b_dn[0].wait_recv()
    half_squares(NEXT, 0, half)
    blocks([NEXT], [q, q_sib, q_oth, q_osib], 0, half, step=4)
    own_v.wait()
    v1r.wait_recv()
    v2r.wait_recv()
    go(v3)
    b_up[1].wait_recv()
    b_dn[1].wait_recv()
    half_squares(NEXT, half, half)
    blocks([NEXT], [q, q_sib, q_oth, q_osib], half, half, step=4)

    def gather(buf, me, others, base, send=True, wait=True):
        for i, (_, d) in enumerate(others if send else []):
            go(pltpu.make_async_remote_copy(
                src_ref=buf.at[me], dst_ref=buf.at[me], send_sem=gs.at[base + i], recv_sem=gr.at[base + me],
                device_id=d, device_id_type=pl.DeviceIdType.MESH))
        for p, d in others if wait else []:
            pltpu.make_async_remote_copy(
                src_ref=buf.at[me], dst_ref=buf.at[p], send_sem=gs.at[base], recv_sem=gr.at[base + p],
                device_id=d, device_id_type=pl.DeviceIdType.MESH).wait_recv()

    for s in range(4):
        ldx[s // 2, mine[(0, 2)[s // 2]], :, pl.ds((s % 2) * nl, nl)] = jnp.sum(colacc[s], axis=0, keepdims=True)
    routes = ((0, 2), (2, 0))
    for i, (one, two) in enumerate(routes):
        gather(ldx.at[i], mine[one], groups[one], 8 * i, wait=False)
    for blk in range(4):
        for k in range(4):
            t = jnp.sum(rowacc[blk, rq(k), :].T, axis=0, keepdims=True)
            row, part = (k // 2, k % 2) if blk == OWN else (k % 2, k // 2)
            degs[blk, row:row + 1, part * qr:(part + 1) * qr] = t
    dsrc = [(NEAR, 0, 0, 0, down), (NEAR, 1, 1, 1, up), (NEXT, 0, 0, 1, down), (NEXT, 1, 1, 0, up),
            (FAR, 0, 2, 0, far), (FAR, 1, 2, 1, far)]
    for i, (one, two) in enumerate(routes):
        gather(ldx.at[i], mine[one], groups[one], 8 * i, send=False)
        tot = ldx[i, 0]
        for k in range(1, GROUP):
            tot = tot + ldx[i, k]
        ldz[i, pos[two]] = tot
        gather(ldz.at[i], pos[two], lines[two], 16 + 4 * i, wait=False)
    dcp = []
    for i, (blk, row, slot, h, d) in enumerate(dsrc):
        dcp.append(rc(28 + i, degs.at[blk, pl.ds(row, 1)], degr.at[slot, pl.ds(h, 1)], d))
        go(dcp[-1])
    for i, (one, two) in enumerate(routes):
        gather(ldz.at[i], pos[two], lines[two], 16 + 4 * i, send=False)
        tot = ldz[i, 0]
        for k in range(1, NZ):
            tot = tot + ldz[i, k]
        rsv[:, pl.ds(i * 2 * nl, 2 * nl)] = lax.rsqrt(tot)

    v0r.wait_recv()
    v3r.wait_recv()

    def product(blk, acc, r0=0, m=rows):
        part = None
        for s in range(4):
            for k in range(0, nl, 256):
                for w in range(k, k + 256, 128):
                    rv = jnp.broadcast_to(rsv[:, pl.ds(s * nl + w, 128)], (RC, 128))
                    for r in range(r0, r0 + m, RC):
                        scl[pl.ds(r, RC), pl.ds(w, 128)] = (kmat[blk, s, pl.ds(r, RC), pl.ds(w, 128)] * rv).astype(bf16)
                d = jnp.dot(scl[pl.ds(r0, m), pl.ds(k, 256)], evs[s, pl.ds(k, 256), :], preferred_element_type=f32)
                part = d if part is None else part + d
        acc[pl.ds(r0, m)] = part

    def send_part(n, h, d, k, add=None):
        v = acc[rq(2 * k + h)]
        if add is not None:
            v = v + precv[add, rq(k)].astype(f32)
        psend[n, rq(k)] = v.astype(psend.dtype)
        cp = rc(34 + 2 * n + k, psend.at[n, rq(k)], precv.at[n, rq(k)], d)
        go(cp)
        return cp

    first = []
    for k in range(2):
        product(FAR, acc, k * half, half)
        first.append((send_part(0, 0, up, k), send_part(1, 1, down, k)))
    product(NEAR, acc)
    last = []
    for k in range(2):
        last += [send_part(2, 0, down, k), send_part(3, 1, up, k)]
    product(NEXT, acc)
    product(OWN, acc2)
    for k in range(2):
        first[k][0].wait_recv()
        last.append(send_part(4, 1, up, k, 0))
        first[k][1].wait_recv()
        last.append(send_part(5, 0, down, k, 1))

    nrows, nlands = float(NROWS), float(LANDMARKS)
    factor = (nrows * nlands) ** 0.5
    for cp in dcp:
        cp.wait_recv()
    for cp in last:
        cp.wait_recv()
    inv = 1.0 / eigvals[...]
    for h in range(2):
        deg = degs[OWN, h:h + 1, :]
        for k in range(3):
            deg = deg + degr[k, h:h + 1, :]
        f = factor / jnp.sqrt(deg)
        col = jnp.broadcast_to(f, (128, halfr)).T
        for w in range(0, 256, 128):
            v = acc2[pl.ds(h * halfr, halfr), pl.ds(w, 128)] + precv[2 + h, :, pl.ds(w, 128)].astype(f32)
            v = v + precv[4 + h, :, pl.ds(w, 128)].astype(f32)
            coords[pl.ds(h * halfr, halfr), pl.ds(w, 128)] = v * col * inv[:, w:w + 128]

    out_c = pltpu.make_async_copy(coords, coords_out, loc.at[3])
    out_c.start()

    cv = coords[...]
    top = cv.astype(bf16)
    low = (cv - top.astype(f32)).astype(bf16)
    topt, lowt = top.T, low.T
    for i, (a, b) in enumerate(((0, 0), (0, 128), (128, 128))):
        v = jnp.dot(topt[a:a + 128], top[:, b:b + 128], preferred_element_type=f32)
        v = v + jnp.dot(topt[a:a + 128], low[:, b:b + 128], preferred_element_type=f32)
        v = v + jnp.dot(lowt[a:a + 128], top[:, b:b + 128], preferred_element_type=f32)
        gpart[i] = v.reshape(gpart.shape[1:])
    for i in range(3):
        g = mine[i]
        for j, (p, d) in enumerate(groups[i]):
            go(pltpu.make_async_remote_copy(
                src_ref=gpart.at[i, p], dst_ref=grx.at[i, g], send_sem=gs.at[24 + 8 * i + j], recv_sem=gr.at[24 + 8 * i + g],
                device_id=d, device_id_type=pl.DeviceIdType.MESH))
    for i in range(3):
        two = (i + 1) % 3
        for p, d in groups[i]:
            pltpu.make_async_remote_copy(
                src_ref=gpart.at[i, p], dst_ref=grx.at[i, p], send_sem=gs.at[24 + 8 * i], recv_sem=gr.at[24 + 8 * i + p],
                device_id=d, device_id_type=pl.DeviceIdType.MESH).wait_recv()
        tot = gpart[i, mine[i]]
        for p, _ in groups[i]:
            tot = tot + grx[i, p]
        gry[i, pos[two]] = tot
        gather(gry.at[i], pos[two], lines[two], 48 + 4 * i, wait=False)
    for i in range(3):
        two, three = (i + 1) % 3, (i + 2) % 3
        gather(gry.at[i], pos[two], lines[two], 48 + 4 * i, send=False)
        tot = gry[i, 0]
        for k in range(1, NY):
            tot = tot + gry[i, k]
        grz[i, pos[three]] = tot
        gather(grz.at[i], pos[three], lines[three], 60 + 4 * i, wait=False)
    for i in range(3):
        three = (i + 2) % 3
        gather(grz.at[i], pos[three], lines[three], 60 + 4 * i, send=False)
        tot = grz[i, 0]
        for k in range(1, NZ):
            tot = tot + grz[i, k]
        gfull[i, mine[i]] = tot * (1.0 / NROWS)
        gather(gfull.at[i], mine[i], groups[i], 72 + 8 * i, wait=False)
    for i, (a, b) in enumerate(((0, 0), (0, 128), (128, 128))):
        gather(gfull.at[i], mine[i], groups[i], 72 + 8 * i, send=False)
        v = gfull[i].reshape(128, 128)
        gram[a:a + 128, b:b + 128] = v
        if a != b:
            gram[b:b + 128, a:a + 128] = v.T

    out_g = pltpu.make_async_copy(gram, gram_out, loc.at[4])
    out_g.start()
    for cp in sends:
        cp.wait_send()
    out_c.wait()
    out_g.wait()

def copy_out(c, g, c_out, g_out, c_buf, g_buf, sem):
    parts = [(c, c_buf, c_out, k) for k in range(4)] + [(g, g_buf, g_out, k) for k in range(2)]
    cin, cout = [], []
    for i, (src, buf, dst, k) in enumerate(parts):
        at = pl.ds(k * 128, 128)
        cin.append(pltpu.make_async_copy(src.at[at], buf.at[at], sem.at[2 * i]))
        cout.append(pltpu.make_async_copy(buf.at[at], dst.at[at], sem.at[2 * i + 1]))
        cin[-1].start()
    for a, b in zip(cin, cout):
        a.wait()
        b.start()
    for b in cout:
        b.wait()


NROWS, LANDMARKS = 65536, 16384


def per_device(items, landmarks, scales, eigvecs, eigvals):
    rows, dim = items.shape
    nl, width = eigvecs.shape
    half = rows // 2
    anyspec = pl.BlockSpec(memory_space=pl.ANY)
    vspec = pl.BlockSpec(memory_space=pltpu.VMEM)
    V, DMA = pltpu.VMEM, pltpu.SemaphoreType.DMA
    shapes = (jax.ShapeDtypeStruct((rows, width), f32), jax.ShapeDtypeStruct((width, width), f32))
    results = pl.pallas_call(
        kernel,
        out_shape=shapes,
        in_specs=[anyspec, anyspec, anyspec, vspec, vspec],
        out_specs=(anyspec, anyspec),
        scratch_shapes=[
            V((rows, width), f32), V((width, width), f32),
            V((4, rows, dim), bf16), V((4, nl, dim), bf16), V((4, nl, width), bf16), V((4, 8, nl), f32),
            V((4, rows, 128), f32), V((4, 4, rows, nl), f32), V((4, rows, 128), f32), V((4, 8, nl), f32),
            V((2, rows, NTILE), f32),
            V((2, GROUP, 1, 2 * nl), f32), V((2, NZ, 1, 2 * nl), f32), V((1, 4 * nl), f32), V((4, 2, half), f32), V((3, 2, half), f32),
            V((rows, nl), bf16), V((rows, width), f32), V((rows, width), f32), V((6, half, width), PT), V((6, half, width), PT),
            V((3, GROUP, 16, 128), f32), V((3, GROUP, 16, 128), f32), V((3, NY, 16, 128), f32), V((3, NZ, 16, 128), f32),
            V((3, GROUP, 16, 128), f32),
            DMA((5,)), DMA((46,)), DMA((46,)), DMA((96,)), DMA((96,)),
        ],
        compiler_params=pltpu.CompilerParams(collective_id=0, has_side_effects=True, vmem_limit_bytes=62 * 2**20),
    )(items, landmarks, eigvecs, scales.reshape(1, nl), eigvals.reshape(1, width))
    return pl.pallas_call(
        copy_out, out_shape=shapes, in_specs=[anyspec, anyspec], out_specs=(anyspec, anyspec),
        scratch_shapes=[V((rows, width), f32), V((width, width), f32), DMA((12,))])(*results)


def solution(mesh):
    return jax.shard_map(
        per_device, mesh=mesh,
        in_specs=(P(("dp", "land"), None), P("land", None), P("land"), P("land", None), P()),
        out_specs=(P(("dp", "land"), None), P()), check_vma=False)
```

```python
import jax
import jax.numpy as jnp
from jax import lax
from jax.experimental import pallas as pl
from jax.experimental.pallas import tpu as pltpu
from jax.sharding import PartitionSpec as P


f32, bf16 = jnp.float32, jnp.bfloat16
LOG2E = 1.4426950408889634
PT = jnp.bfloat16
NTILE = 512
OWN, NEAR, NEXT, FAR = 0, 1, 2, 3
NX = NY = NZ = 4
GROUP = 8


def place(x, y, z, c):
    return {"dp": lax.div(z, 2) * NX + x, "land": lax.rem(z, 2) * 8 + y * 2 + c}


def kernel(items, lands, vecs, scales, eigvals, coords_out, gram_out, coords, gram,
           it, lmk, evs, lp, rh, kmat, rowacc, colacc, cross,
           ldx, ldz, rsv, degs, degr, scl, acc, acc2, psend, precv,
           gpart, grx, gry, grz, gfull,
           loc, ssem, rsem, gs, gr):
    rows, halfr = items.shape[0], items.shape[0] // 2
    nl = lands.shape[0]
    halfl = nl // 2
    dp, land = lax.axis_index("dp"), lax.axis_index("land")
    x, zh = lax.rem(dp, NX), lax.div(dp, NX)
    c, y, zl = lax.rem(land, 2), lax.rem(lax.div(land, 2), NY), lax.div(land, 8)
    z = zh * 2 + zl
    yn, yp = lax.rem(y + 1, NY), lax.rem(y + NY - 1, NY)
    zn, zp = lax.rem(z + 1, NZ), lax.rem(z + NZ - 1, NZ)
    yfar = lax.rem(y + 2, NY)
    up, down, far = place(x, yn, z, c), place(x, yp, z, c), place(x, yfar, z, c)
    zup, zdown = place(x, y, zn, c), place(x, y, zp, c)
    sib = place(x, y, z, 1 - c)
    pos = (x, y, z)

    def at(axis, v, core):
        v = [v if k == axis else pos[k] for k in range(3)]
        return place(*v, core)

    groups, lines, mine = [], [], []
    for axis in range(3):
        g = pos[axis] * 2 + c
        mine.append(g)
        groups.append([])
        for k in range(1, GROUP):
            p = lax.rem(g + k, GROUP)
            groups[axis].append((p, at(axis, lax.div(p, 2), lax.rem(p, 2))))
        lines.append([])
        for k in range(1, NX):
            p = lax.rem(pos[axis] + k, NX)
            lines[axis].append((p, at(axis, p, c)))
    q = zl * 2 + c
    q_sib, q_oth, q_osib = zl * 2 + 1 - c, (1 - zl) * 2 + c, (1 - zl) * 2 + 1 - c

    barrier = pltpu.get_barrier_semaphore()
    peers = [sib] + [at(axis, lax.rem(pos[axis] + k, NX), core) for axis in range(3) for k in range(1, NX) for core in (c, 1 - c)]
    for d in peers:
        pl.semaphore_signal(barrier, inc=1, device_id=d, device_id_type=pl.DeviceIdType.MESH)

    own_i = pltpu.make_async_copy(items, it.at[OWN], loc.at[0])
    own_l = pltpu.make_async_copy(lands, lmk.at[q], loc.at[1])
    own_v = pltpu.make_async_copy(vecs, evs.at[q], loc.at[2])
    own_l.start()
    own_i.start()
    own_v.start()

    sends = []

    def rc(i, src, dst, d):
        return pltpu.make_async_remote_copy(
            src_ref=src, dst_ref=dst, send_sem=ssem.at[i], recv_sem=rsem.at[i],
            device_id=d, device_id_type=pl.DeviceIdType.MESH)

    def go(cp):
        cp.start()
        sends.append(cp)

    qr, ql = rows // 4, nl // 4

    def rq(k, n=1):
        return pl.ds(k * qr, n * qr)

    def lq(k):
        return pl.ds(k * ql, ql)

    a_up = [rc(k, items.at[rq(k)], it.at[NEAR, rq(2 * k)], up) for k in range(2)]
    a_dn = [rc(2 + k, items.at[rq(2 + k)], it.at[NEAR, rq(2 * k + 1)], down) for k in range(2)]
    f_up = [rc(4 + k, it.at[NEAR, rq(2 * k)], it.at[FAR, rq(2 * k)], up) for k in range(2)]
    f_dn = [rc(6 + k, it.at[NEAR, rq(2 * k + 1)], it.at[FAR, rq(2 * k + 1)], down) for k in range(2)]
    b_up = [rc(8 + k, items.at[rq(2 + k)], it.at[NEXT, rq(2 * k)], up) for k in range(2)]
    b_dn = [rc(10 + k, items.at[rq(k)], it.at[NEXT, rq(2 * k + 1)], down) for k in range(2)]
    zdev = [zup, zdown, zup, zdown]
    l_z = [rc(12 + k, lands.at[lq(k)], lmk.at[q, lq(k)], zdev[k]) for k in range(4)]
    l_zr = [rc(12 + k, lands.at[lq(k)], lmk.at[q_oth, lq(k)], zdev[k]) for k in range(4)]
    l_f = [rc(16 + k, lmk.at[q_oth, lq(k)], lmk.at[q_oth, lq(k)], sib) for k in range(4)]
    l_fr = [rc(16 + k, lmk.at[q_oth, lq(k)], lmk.at[q_osib, lq(k)], sib) for k in range(4)]
    l0 = rc(20, lands, lmk.at[q], sib)
    l0r = rc(20, lands, lmk.at[q_sib], sib)
    p0 = rc(21, lp.at[q], lp.at[q], sib)
    p0r = rc(21, lp.at[q], lp.at[q_sib], sib)
    p1 = rc(22, lp.at[q], lp.at[q], zup)
    p1r = rc(22, lp.at[q], lp.at[q_oth], zup)
    p2 = rc(23, lp.at[q_oth], lp.at[q_oth], sib)
    p2r = rc(23, lp.at[q_oth], lp.at[q_osib], sib)
    llo, lhi = pl.ds(0, halfl), pl.ds(halfl, halfl)
    v0 = rc(24, vecs, evs.at[q], sib)
    v0r = rc(24, vecs, evs.at[q_sib], sib)
    v1 = rc(25, vecs.at[llo], evs.at[q, llo], zup)
    v1r = rc(25, vecs.at[llo], evs.at[q_oth, llo], zup)
    v2 = rc(26, vecs.at[lhi], evs.at[q, lhi], zdown)
    v2r = rc(26, vecs.at[lhi], evs.at[q_oth, lhi], zdown)
    v3 = rc(27, evs.at[q_oth], evs.at[q_oth], sib)
    v3r = rc(27, evs.at[q_oth], evs.at[q_osib], sib)

    own_l.wait()
    for r in range(0, nl, 128):
        part = None
        for k in range(0, lands.shape[1], 128):
            v = lmk[q, pl.ds(r, 128), pl.ds(k, 128)].astype(f32)
            part = v * v if part is None else part + v * v
        sq = jnp.sum(part.T, axis=0, keepdims=True)
        s = scales[:, pl.ds(r, 128)] * LOG2E
        lp[q, 0:1, pl.ds(r, 128)] = s + s
        lp[q, 1:2, pl.ds(r, 128)] = -s * sq
        lp[q, 2:8, pl.ds(r, 128)] = jnp.zeros((6, 128), f32)

    pl.semaphore_wait(barrier, len(peers))
    for cp in a_up + a_dn:
        go(cp)
    go(p1)
    go(l0)
    go(p0)
    for cp in l_z:
        go(cp)

    colacc[...] = jnp.zeros_like(colacc)
    rowacc[...] = jnp.zeros_like(rowacc)

    def half_squares(blk, r0, n):
        for r in range(r0, r0 + n, 128):
            part = None
            for k in range(0, items.shape[1], 128):
                v = it[blk, pl.ds(r, 128), pl.ds(k, 128)].astype(f32)
                part = v * v if part is None else part + v * v
            rh[blk, pl.ds(r, 128), :] = jnp.broadcast_to(0.5 * jnp.sum(part, axis=1, keepdims=True), (128, 128))

    NT, RC = NTILE, 64

    def block(blk, slot, r0, m, n0, nn):
        for n in range(n0, n0 + nn, NT):
            buf = (n // NT) % 2
            cross[buf, pl.ds(0, m)] = lax.dot_general(
                it[blk, pl.ds(r0, m), :], lmk[slot, pl.ds(n, NT), :], (((1,), (1,)), ((), ())), preferred_element_type=f32)
            col = [None] * (NT // 128)
            for r in range(0, m, RC):
                half_sq = rh[blk, pl.ds(r0 + r, RC), :]
                row = None
                for w in range(NT // 128):
                    cols = pl.ds(n + w * 128, 128)
                    t = (cross[buf, pl.ds(r, RC), pl.ds(w * 128, 128)] - half_sq) * lp[slot, 0:1, cols] + lp[slot, 1:2, cols]
                    kv = jnp.exp2(t)
                    kmat[blk, slot, pl.ds(r0 + r, RC), cols] = kv
                    row = kv if row is None else row + kv
                    ks = jnp.sum(kv.reshape(RC // 8, 8, 128), axis=0)
                    col[w] = ks if col[w] is None else col[w] + ks
                rowacc[blk, pl.ds(r0 + r, RC), :] += row
            for w in range(NT // 128):
                colacc[slot, :, pl.ds(n + w * 128, 128)] += col[w]

    def blocks(blks, slots, r0=0, m=rows, n0=0, nn=nl, step=1):
        pairs = [(b, s) for b in blks for s in slots]
        n = len(pairs)

        def pick(t, values):
            out = values[-1]
            for i in range(n - 2, -1, -1):
                out = jnp.where(t == i, values[i], out)
            return out

        @pl.loop(0, n // step)
        def _(t0):
            for u in range(step):
                t = t0 * step + u
                block(pick(t, [jnp.int32(b) for b, _ in pairs]), pick(t, [s for _, s in pairs]), r0, m, n0, nn)

    half = rows // 2
    own_i.wait()
    half_squares(OWN, 0, rows)
    blocks([OWN], [q])
    a_up[0].wait_recv()
    go(f_up[0])
    a_dn[0].wait_recv()
    go(f_dn[0])
    l0r.wait_recv()
    p0r.wait_recv()
    blocks([OWN], [q_sib])
    a_up[1].wait_recv()
    go(f_up[1])
    a_dn[1].wait_recv()
    go(f_dn[1])
    for cp in b_up + b_dn:
        go(cp)
    half_squares(NEAR, 0, rows)
    p1r.wait_recv()
    go(p2)
    l_zr[0].wait_recv()
    go(l_f[0])
    l_zr[1].wait_recv()
    go(l_f[1])
    go(v1)
    go(v2)
    go(v0)
    lh = nl // 2
    blocks([NEAR], [q, q_sib], step=2)
    blocks([OWN, NEAR], [q_oth], 0, rows, 0, lh, step=2)
    p2r.wait_recv()
    l_fr[0].wait_recv()
    l_fr[1].wait_recv()
    blocks([OWN, NEAR], [q_osib], 0, rows, 0, lh, step=2)
    f_up[0].wait_recv()
    f_dn[0].wait_recv()
    half_squares(FAR, 0, half)
    blocks([FAR], [q, q_sib], 0, half, step=2)
    blocks([FAR], [q_oth, q_osib], 0, half, 0, lh, step=2)
    l_zr[2].wait_recv()
    go(l_f[2])
    l_zr[3].wait_recv()
    go(l_f[3])
    blocks([OWN, NEAR], [q_oth], 0, rows, lh, lh, step=2)
    blocks([FAR], [q_oth], 0, half, lh, lh)
    f_up[1].wait_recv()
    f_dn[1].wait_recv()
    half_squares(FAR, half, half)
    l_fr[2].wait_recv()
    l_fr[3].wait_recv()
    blocks([FAR], [q, q_sib, q_oth, q_osib], half, half, step=4)
    blocks([FAR], [q_osib], 0, half, lh, lh)
    blocks([OWN, NEAR], [q_osib], 0, rows, lh, lh, step=2)
    b_up[0].wait_recv()
    b_dn[0].wait_recv()
    half_squares(NEXT, 0, half)
    blocks([NEXT], [q, q_sib, q_oth, q_osib], 0, half, step=4)
    own_v.wait()
    v1r.wait_recv()
    v2r.wait_recv()
    go(v3)
    b_up[1].wait_recv()
    b_dn[1].wait_recv()
    half_squares(NEXT, half, half)
    blocks([NEXT], [q, q_sib, q_oth, q_osib], half, half, step=4)

    def gather(buf, me, others, base, send=True, wait=True):
        for i, (_, d) in enumerate(others if send else []):
            go(pltpu.make_async_remote_copy(
                src_ref=buf.at[me], dst_ref=buf.at[me], send_sem=gs.at[base + i], recv_sem=gr.at[base + me],
                device_id=d, device_id_type=pl.DeviceIdType.MESH))
        for p, d in others if wait else []:
            pltpu.make_async_remote_copy(
                src_ref=buf.at[me], dst_ref=buf.at[p], send_sem=gs.at[base], recv_sem=gr.at[base + p],
                device_id=d, device_id_type=pl.DeviceIdType.MESH).wait_recv()

    for s in range(4):
        ldx[s // 2, mine[(0, 2)[s // 2]], :, pl.ds((s % 2) * nl, nl)] = jnp.sum(colacc[s], axis=0, keepdims=True)
    routes = ((0, 2), (2, 0))
    for i, (one, two) in enumerate(routes):
        gather(ldx.at[i], mine[one], groups[one], 8 * i, wait=False)
    for blk in range(4):
        for k in range(4):
            t = jnp.sum(rowacc[blk, rq(k), :].T, axis=0, keepdims=True)
            row, part = (k // 2, k % 2) if blk == OWN else (k % 2, k // 2)
            degs[blk, row:row + 1, part * qr:(part + 1) * qr] = t
    dsrc = [(NEAR, 0, 0, 0, down), (NEAR, 1, 1, 1, up), (NEXT, 0, 0, 1, down), (NEXT, 1, 1, 0, up),
            (FAR, 0, 2, 0, far), (FAR, 1, 2, 1, far)]
    for i, (one, two) in enumerate(routes):
        gather(ldx.at[i], mine[one], groups[one], 8 * i, send=False)
        tot = ldx[i, 0]
        for k in range(1, GROUP):
            tot = tot + ldx[i, k]
        ldz[i, pos[two]] = tot
        gather(ldz.at[i], pos[two], lines[two], 16 + 4 * i, wait=False)
    dcp = []
    for i, (blk, row, slot, h, d) in enumerate(dsrc):
        dcp.append(rc(28 + i, degs.at[blk, pl.ds(row, 1)], degr.at[slot, pl.ds(h, 1)], d))
        go(dcp[-1])
    for i, (one, two) in enumerate(routes):
        gather(ldz.at[i], pos[two], lines[two], 16 + 4 * i, send=False)
        tot = ldz[i, 0]
        for k in range(1, NZ):
            tot = tot + ldz[i, k]
        rsv[:, pl.ds(i * 2 * nl, 2 * nl)] = lax.rsqrt(tot)

    v0r.wait_recv()
    v3r.wait_recv()

    def product(blk, acc, r0=0, m=rows):
        part = None
        for s in range(4):
            for k in range(0, nl, 256):
                for w in range(k, k + 256, 128):
                    rv = jnp.broadcast_to(rsv[:, pl.ds(s * nl + w, 128)], (RC, 128))
                    for r in range(r0, r0 + m, RC):
                        scl[pl.ds(r, RC), pl.ds(w, 128)] = (kmat[blk, s, pl.ds(r, RC), pl.ds(w, 128)] * rv).astype(bf16)
                d = jnp.dot(scl[pl.ds(r0, m), pl.ds(k, 256)], evs[s, pl.ds(k, 256), :], preferred_element_type=f32)
                part = d if part is None else part + d
        acc[pl.ds(r0, m)] = part

    def send_part(n, h, d, k, add=None):
        v = acc[rq(2 * k + h)]
        if add is not None:
            v = v + precv[add, rq(k)].astype(f32)
        psend[n, rq(k)] = v.astype(psend.dtype)
        cp = rc(34 + 2 * n + k, psend.at[n, rq(k)], precv.at[n, rq(k)], d)
        go(cp)
        return cp

    first = []
    for k in range(2):
        product(FAR, acc, k * half, half)
        first.append((send_part(0, 0, up, k), send_part(1, 1, down, k)))
    product(NEAR, acc)
    last = [[send_part(2, 0, down, k), send_part(3, 1, up, k)] for k in range(2)]
    product(NEXT, acc)
    product(OWN, acc2)
    for k in range(2):
        first[k][0].wait_recv()
        last[k].append(send_part(4, 1, up, k, 0))
        first[k][1].wait_recv()
        last[k].append(send_part(5, 0, down, k, 1))

    nrows, nlands = float(NROWS), float(LANDMARKS)
    factor = (nrows * nlands) ** 0.5
    for cp in dcp:
        cp.wait_recv()
    inv = 1.0 / eigvals[...]
    cols = []
    for h in range(2):
        deg = degs[OWN, h:h + 1, :]
        for k in range(3):
            deg = deg + degr[k, h:h + 1, :]
        cols.append(jnp.broadcast_to(factor / jnp.sqrt(deg), (128, half)).T)
    for k in range(2):
        for cp in last[k]:
            cp.wait_recv()
        tops, lows = [], []
        for h in range(2):
            v = acc2[rq(2 * h + k)] + precv[2 + h, rq(k)].astype(f32) + precv[4 + h, rq(k)].astype(f32)
            col = cols[h][k * qr:(k + 1) * qr]
            v = jnp.concatenate([v[:, w:w + 128] * col for w in range(0, v.shape[1], 128)], axis=1) * inv
            coords[rq(2 * h + k)] = v
            tops.append(v.astype(bf16))
            lows.append((v - tops[-1].astype(f32)).astype(bf16))
        top, low = jnp.concatenate(tops, axis=0), jnp.concatenate(lows, axis=0)
        topt, lowt = top.T, low.T
        for i, (a, b) in enumerate(((0, 0), (0, 128), (128, 128))):
            v = jnp.dot(topt[a:a + 128], top[:, b:b + 128], preferred_element_type=f32)
            v = v + jnp.dot(topt[a:a + 128], low[:, b:b + 128], preferred_element_type=f32)
            v = v + jnp.dot(lowt[a:a + 128], top[:, b:b + 128], preferred_element_type=f32)
            v = v.reshape(gpart.shape[1:])
            gpart[i] = v if k == 0 else gpart[i] + v
    out_c = pltpu.make_async_copy(coords, coords_out, loc.at[3])
    out_c.start()
    for i in range(3):
        g = mine[i]
        for j, (p, d) in enumerate(groups[i]):
            go(pltpu.make_async_remote_copy(
                src_ref=gpart.at[i, p], dst_ref=grx.at[i, g], send_sem=gs.at[24 + 8 * i + j], recv_sem=gr.at[24 + 8 * i + g],
                device_id=d, device_id_type=pl.DeviceIdType.MESH))
    for i in range(3):
        two = (i + 1) % 3
        for p, d in groups[i]:
            pltpu.make_async_remote_copy(
                src_ref=gpart.at[i, p], dst_ref=grx.at[i, p], send_sem=gs.at[24 + 8 * i], recv_sem=gr.at[24 + 8 * i + p],
                device_id=d, device_id_type=pl.DeviceIdType.MESH).wait_recv()
        tot = gpart[i, mine[i]]
        for p, _ in groups[i]:
            tot = tot + grx[i, p]
        gry[i, pos[two]] = tot
        gather(gry.at[i], pos[two], lines[two], 48 + 4 * i, wait=False)
    for i in range(3):
        two, three = (i + 1) % 3, (i + 2) % 3
        gather(gry.at[i], pos[two], lines[two], 48 + 4 * i, send=False)
        tot = gry[i, 0]
        for k in range(1, NY):
            tot = tot + gry[i, k]
        grz[i, pos[three]] = tot
        gather(grz.at[i], pos[three], lines[three], 60 + 4 * i, wait=False)
    for i in range(3):
        three = (i + 2) % 3
        gather(grz.at[i], pos[three], lines[three], 60 + 4 * i, send=False)
        tot = grz[i, 0]
        for k in range(1, NZ):
            tot = tot + grz[i, k]
        gfull[i, mine[i]] = tot * (1.0 / NROWS)
        gather(gfull.at[i], mine[i], groups[i], 72 + 8 * i, wait=False)
    for i, (a, b) in enumerate(((0, 0), (0, 128), (128, 128))):
        gather(gfull.at[i], mine[i], groups[i], 72 + 8 * i, send=False)
        v = gfull[i].reshape(128, 128)
        gram[a:a + 128, b:b + 128] = v
        if a != b:
            gram[b:b + 128, a:a + 128] = v.T

    out_g = pltpu.make_async_copy(gram, gram_out, loc.at[4])
    out_g.start()
    for cp in sends:
        cp.wait_send()
    out_c.wait()
    out_g.wait()

def copy_out(c, g, c_out, g_out, c_buf, g_buf, sem):
    parts = [(c, c_buf, c_out, k) for k in range(4)] + [(g, g_buf, g_out, k) for k in range(2)]
    cin, cout = [], []
    for i, (src, buf, dst, k) in enumerate(parts):
        at = pl.ds(k * 128, 128)
        cin.append(pltpu.make_async_copy(src.at[at], buf.at[at], sem.at[2 * i]))
        cout.append(pltpu.make_async_copy(buf.at[at], dst.at[at], sem.at[2 * i + 1]))
        cin[-1].start()
    for a, b in zip(cin, cout):
        a.wait()
        b.start()
    for b in cout:
        b.wait()


NROWS, LANDMARKS = 65536, 16384


def per_device(items, landmarks, scales, eigvecs, eigvals):
    rows, dim = items.shape
    nl, width = eigvecs.shape
    half = rows // 2
    anyspec = pl.BlockSpec(memory_space=pl.ANY)
    vspec = pl.BlockSpec(memory_space=pltpu.VMEM)
    V, DMA = pltpu.VMEM, pltpu.SemaphoreType.DMA
    shapes = (jax.ShapeDtypeStruct((rows, width), f32), jax.ShapeDtypeStruct((width, width), f32))
    results = pl.pallas_call(
        kernel,
        out_shape=shapes,
        in_specs=[anyspec, anyspec, anyspec, vspec, vspec],
        out_specs=(anyspec, anyspec),
        scratch_shapes=[
            V((rows, width), f32), V((width, width), f32),
            V((4, rows, dim), bf16), V((4, nl, dim), bf16), V((4, nl, width), bf16), V((4, 8, nl), f32),
            V((4, rows, 128), f32), V((4, 4, rows, nl), f32), V((4, rows, 128), f32), V((4, 8, nl), f32),
            V((2, rows, NTILE), f32),
            V((2, GROUP, 1, 2 * nl), f32), V((2, NZ, 1, 2 * nl), f32), V((1, 4 * nl), f32), V((4, 2, half), f32), V((3, 2, half), f32),
            V((rows, nl), bf16), V((rows, width), f32), V((rows, width), f32), V((6, half, width), PT), V((6, half, width), PT),
            V((3, GROUP, 16, 128), f32), V((3, GROUP, 16, 128), f32), V((3, NY, 16, 128), f32), V((3, NZ, 16, 128), f32),
            V((3, GROUP, 16, 128), f32),
            DMA((5,)), DMA((46,)), DMA((46,)), DMA((96,)), DMA((96,)),
        ],
        compiler_params=pltpu.CompilerParams(collective_id=0, has_side_effects=True, vmem_limit_bytes=62 * 2**20),
    )(items, landmarks, eigvecs, scales.reshape(1, nl), eigvals.reshape(1, width))
    return pl.pallas_call(
        copy_out, out_shape=shapes, in_specs=[anyspec, anyspec], out_specs=(anyspec, anyspec),
        scratch_shapes=[V((rows, width), f32), V((width, width), f32), DMA((12,))])(*results)


def solution(mesh):
    return jax.shard_map(
        per_device, mesh=mesh,
        in_specs=(P(("dp", "land"), None), P("land", None), P("land"), P("land", None), P()),
        out_specs=(P(("dp", "land"), None), P()), check_vma=False)
```

```python
import jax
import jax.numpy as jnp
from jax import lax
from jax.experimental import pallas as pl
from jax.experimental.pallas import tpu as pltpu
from jax.sharding import PartitionSpec as P


f32, bf16 = jnp.float32, jnp.bfloat16
LOG2E = 1.4426950408889634
PT = jnp.bfloat16
NTILE = 512
OWN, NEAR, NEXT, FAR = 0, 1, 2, 3
NX = NY = NZ = 4
GROUP = 8


def place(x, y, z, c):
    return {"dp": lax.div(z, 2) * NX + x, "land": lax.rem(z, 2) * 8 + y * 2 + c}


def kernel(items, lands, vecs, scales, eigvals, coords_out, gram_out, coords, gram,
           it, lmk, evs, lp, rh, kmat, rowacc, colacc, cross,
           ldx, ldz, rsv, degs, degr, scl, acc, acc2, psend, precv,
           gpart, grx, gry, grz, gfull,
           loc, ssem, rsem, gs, gr):
    rows, halfr = items.shape[0], items.shape[0] // 2
    nl = lands.shape[0]
    halfl = nl // 2
    dp, land = lax.axis_index("dp"), lax.axis_index("land")
    x, zh = lax.rem(dp, NX), lax.div(dp, NX)
    c, y, zl = lax.rem(land, 2), lax.rem(lax.div(land, 2), NY), lax.div(land, 8)
    z = zh * 2 + zl
    yn, yp = lax.rem(y + 1, NY), lax.rem(y + NY - 1, NY)
    zn, zp = lax.rem(z + 1, NZ), lax.rem(z + NZ - 1, NZ)
    yfar = lax.rem(y + 2, NY)
    up, down, far = place(x, yn, z, c), place(x, yp, z, c), place(x, yfar, z, c)
    zup, zdown = place(x, y, zn, c), place(x, y, zp, c)
    sib = place(x, y, z, 1 - c)
    pos = (x, y, z)

    def at(axis, v, core):
        v = [v if k == axis else pos[k] for k in range(3)]
        return place(*v, core)

    groups, lines, mine = [], [], []
    for axis in range(3):
        g = pos[axis] * 2 + c
        mine.append(g)
        groups.append([])
        for k in range(1, GROUP):
            p = lax.rem(g + k, GROUP)
            groups[axis].append((p, at(axis, lax.div(p, 2), lax.rem(p, 2))))
        lines.append([])
        for k in range(1, NX):
            p = lax.rem(pos[axis] + k, NX)
            lines[axis].append((p, at(axis, p, c)))
    q = zl * 2 + c
    q_sib, q_oth, q_osib = zl * 2 + 1 - c, (1 - zl) * 2 + c, (1 - zl) * 2 + 1 - c

    barrier = pltpu.get_barrier_semaphore()
    peers = [sib] + [at(axis, lax.rem(pos[axis] + k, NX), core) for axis in range(3) for k in range(1, NX) for core in (c, 1 - c)]
    for d in peers:
        pl.semaphore_signal(barrier, inc=1, device_id=d, device_id_type=pl.DeviceIdType.MESH)

    own_i = pltpu.make_async_copy(items, it.at[OWN], loc.at[0])
    own_l = pltpu.make_async_copy(lands, lmk.at[q], loc.at[1])
    own_v = pltpu.make_async_copy(vecs, evs.at[q], loc.at[2])
    own_l.start()
    own_i.start()
    own_v.start()

    sends = []

    def rc(i, src, dst, d):
        return pltpu.make_async_remote_copy(
            src_ref=src, dst_ref=dst, send_sem=ssem.at[i], recv_sem=rsem.at[i],
            device_id=d, device_id_type=pl.DeviceIdType.MESH)

    def go(cp):
        cp.start()
        sends.append(cp)

    qr, ql = rows // 4, nl // 4

    def rq(k, n=1):
        return pl.ds(k * qr, n * qr)

    def lq(k):
        return pl.ds(k * ql, ql)

    a_up = [rc(k, items.at[rq(k)], it.at[NEAR, rq(2 * k)], up) for k in range(2)]
    a_dn = [rc(2 + k, items.at[rq(2 + k)], it.at[NEAR, rq(2 * k + 1)], down) for k in range(2)]
    f_up = [rc(4 + k, it.at[NEAR, rq(2 * k)], it.at[FAR, rq(2 * k)], up) for k in range(2)]
    f_dn = [rc(6 + k, it.at[NEAR, rq(2 * k + 1)], it.at[FAR, rq(2 * k + 1)], down) for k in range(2)]
    b_up = [rc(8 + k, items.at[rq(2 + k)], it.at[NEXT, rq(2 * k)], up) for k in range(2)]
    b_dn = [rc(10 + k, items.at[rq(k)], it.at[NEXT, rq(2 * k + 1)], down) for k in range(2)]
    zdev = [zup, zdown, zup, zdown]
    l_z = [rc(12 + k, lands.at[lq(k)], lmk.at[q, lq(k)], zdev[k]) for k in range(4)]
    l_zr = [rc(12 + k, lands.at[lq(k)], lmk.at[q_oth, lq(k)], zdev[k]) for k in range(4)]
    l_f = [rc(16 + k, lmk.at[q_oth, lq(k)], lmk.at[q_oth, lq(k)], sib) for k in range(4)]
    l_fr = [rc(16 + k, lmk.at[q_oth, lq(k)], lmk.at[q_osib, lq(k)], sib) for k in range(4)]
    l0 = rc(20, lands, lmk.at[q], sib)
    l0r = rc(20, lands, lmk.at[q_sib], sib)
    p0 = rc(21, lp.at[q], lp.at[q], sib)
    p0r = rc(21, lp.at[q], lp.at[q_sib], sib)
    p1 = rc(22, lp.at[q], lp.at[q], zup)
    p1r = rc(22, lp.at[q], lp.at[q_oth], zup)
    p2 = rc(23, lp.at[q_oth], lp.at[q_oth], sib)
    p2r = rc(23, lp.at[q_oth], lp.at[q_osib], sib)
    llo, lhi = pl.ds(0, halfl), pl.ds(halfl, halfl)
    v0 = rc(24, vecs, evs.at[q], sib)
    v0r = rc(24, vecs, evs.at[q_sib], sib)
    v1 = rc(25, vecs.at[llo], evs.at[q, llo], zup)
    v1r = rc(25, vecs.at[llo], evs.at[q_oth, llo], zup)
    v2 = rc(26, vecs.at[lhi], evs.at[q, lhi], zdown)
    v2r = rc(26, vecs.at[lhi], evs.at[q_oth, lhi], zdown)
    v3 = rc(27, evs.at[q_oth], evs.at[q_oth], sib)
    v3r = rc(27, evs.at[q_oth], evs.at[q_osib], sib)

    own_l.wait()
    for r in range(0, nl, 128):
        part = None
        for k in range(0, lands.shape[1], 128):
            v = lmk[q, pl.ds(r, 128), pl.ds(k, 128)].astype(f32)
            part = v * v if part is None else part + v * v
        sq = jnp.sum(part.T, axis=0, keepdims=True)
        s = scales[:, pl.ds(r, 128)] * LOG2E
        lp[q, 0:1, pl.ds(r, 128)] = s + s
        lp[q, 1:2, pl.ds(r, 128)] = -s * sq
        lp[q, 2:8, pl.ds(r, 128)] = jnp.zeros((6, 128), f32)

    pl.semaphore_wait(barrier, len(peers))
    for cp in a_up + a_dn:
        go(cp)
    go(p1)
    go(l0)
    go(p0)
    for cp in l_z:
        go(cp)

    colacc[...] = jnp.zeros_like(colacc)
    rowacc[...] = jnp.zeros_like(rowacc)

    def half_squares(blk, r0, n):
        for r in range(r0, r0 + n, 128):
            part = None
            for k in range(0, items.shape[1], 128):
                v = it[blk, pl.ds(r, 128), pl.ds(k, 128)].astype(f32)
                part = v * v if part is None else part + v * v
            rh[blk, pl.ds(r, 128), :] = jnp.broadcast_to(0.5 * jnp.sum(part, axis=1, keepdims=True), (128, 128))

    NT, RC = NTILE, 64

    def block(blk, slot, r0, m, n0, nn):
        for n in range(n0, n0 + nn, NT):
            buf = (n // NT) % 2
            cross[buf, pl.ds(0, m)] = lax.dot_general(
                it[blk, pl.ds(r0, m), :], lmk[slot, pl.ds(n, NT), :], (((1,), (1,)), ((), ())), preferred_element_type=f32)
            col = [None] * (NT // 128)
            for r in range(0, m, RC):
                half_sq = rh[blk, pl.ds(r0 + r, RC), :]
                row = None
                for w in range(NT // 128):
                    cols = pl.ds(n + w * 128, 128)
                    t = (cross[buf, pl.ds(r, RC), pl.ds(w * 128, 128)] - half_sq) * lp[slot, 0:1, cols] + lp[slot, 1:2, cols]
                    kv = jnp.exp2(t)
                    kmat[blk, slot, pl.ds(r0 + r, RC), cols] = kv
                    row = kv if row is None else row + kv
                    ks = jnp.sum(kv.reshape(RC // 8, 8, 128), axis=0)
                    col[w] = ks if col[w] is None else col[w] + ks
                rowacc[blk, pl.ds(r0 + r, RC), :] += row
            for w in range(NT // 128):
                colacc[slot, :, pl.ds(n + w * 128, 128)] += col[w]

    def blocks(blks, slots, r0=0, m=rows, n0=0, nn=nl, step=1):
        pairs = [(b, s) for b in blks for s in slots]
        n = len(pairs)

        def pick(t, values):
            out = values[-1]
            for i in range(n - 2, -1, -1):
                out = jnp.where(t == i, values[i], out)
            return out

        @pl.loop(0, n // step)
        def _(t0):
            for u in range(step):
                t = t0 * step + u
                block(pick(t, [jnp.int32(b) for b, _ in pairs]), pick(t, [s for _, s in pairs]), r0, m, n0, nn)

    half = rows // 2
    own_i.wait()
    half_squares(OWN, 0, rows)
    blocks([OWN], [q])
    a_up[0].wait_recv()
    go(f_up[0])
    a_dn[0].wait_recv()
    go(f_dn[0])
    l0r.wait_recv()
    p0r.wait_recv()
    blocks([OWN], [q_sib])
    a_up[1].wait_recv()
    go(f_up[1])
    a_dn[1].wait_recv()
    go(f_dn[1])
    for cp in b_up + b_dn:
        go(cp)
    half_squares(NEAR, 0, rows)
    p1r.wait_recv()
    go(p2)
    l_zr[0].wait_recv()
    go(l_f[0])
    l_zr[1].wait_recv()
    go(l_f[1])
    go(v1)
    go(v2)
    go(v0)
    lh = nl // 2
    blocks([NEAR], [q, q_sib], step=2)
    blocks([OWN, NEAR], [q_oth], 0, rows, 0, lh, step=2)
    p2r.wait_recv()
    l_fr[0].wait_recv()
    l_fr[1].wait_recv()
    blocks([OWN, NEAR], [q_osib], 0, rows, 0, lh, step=2)
    f_up[0].wait_recv()
    f_dn[0].wait_recv()
    half_squares(FAR, 0, half)
    blocks([FAR], [q, q_sib], 0, half, step=2)
    blocks([FAR], [q_oth, q_osib], 0, half, 0, lh, step=2)
    l_zr[2].wait_recv()
    go(l_f[2])
    l_zr[3].wait_recv()
    go(l_f[3])
    blocks([OWN, NEAR], [q_oth], 0, rows, lh, lh, step=2)
    blocks([FAR], [q_oth], 0, half, lh, lh)
    f_up[1].wait_recv()
    f_dn[1].wait_recv()
    half_squares(FAR, half, half)
    l_fr[2].wait_recv()
    l_fr[3].wait_recv()
    blocks([FAR], [q, q_sib, q_oth, q_osib], half, half, step=4)
    blocks([FAR], [q_osib], 0, half, lh, lh)
    blocks([OWN, NEAR], [q_osib], 0, rows, lh, lh, step=2)
    b_up[0].wait_recv()
    b_dn[0].wait_recv()
    half_squares(NEXT, 0, half)
    blocks([NEXT], [q, q_sib, q_oth, q_osib], 0, half, step=4)
    own_v.wait()
    v1r.wait_recv()
    v2r.wait_recv()
    go(v3)
    b_up[1].wait_recv()
    b_dn[1].wait_recv()
    half_squares(NEXT, half, half)
    blocks([NEXT], [q, q_sib, q_oth, q_osib], half, half, step=4)

    def gather(buf, me, others, base, send=True, wait=True):
        for i, (_, d) in enumerate(others if send else []):
            go(pltpu.make_async_remote_copy(
                src_ref=buf.at[me], dst_ref=buf.at[me], send_sem=gs.at[base + i], recv_sem=gr.at[base + me],
                device_id=d, device_id_type=pl.DeviceIdType.MESH))
        for p, d in others if wait else []:
            pltpu.make_async_remote_copy(
                src_ref=buf.at[me], dst_ref=buf.at[p], send_sem=gs.at[base], recv_sem=gr.at[base + p],
                device_id=d, device_id_type=pl.DeviceIdType.MESH).wait_recv()

    for s in range(4):
        ldx[s // 2, mine[(0, 2)[s // 2]], :, pl.ds((s % 2) * nl, nl)] = jnp.sum(colacc[s], axis=0, keepdims=True)
    routes = ((0, 2), (2, 0))
    for i, (one, two) in enumerate(routes):
        gather(ldx.at[i], mine[one], groups[one], 8 * i, wait=False)
    for blk in range(4):
        for k in range(4):
            t = jnp.sum(rowacc[blk, rq(k), :].T, axis=0, keepdims=True)
            row, part = (k // 2, k % 2) if blk == OWN else (k % 2, k // 2)
            degs[blk, row:row + 1, part * qr:(part + 1) * qr] = t
    dsrc = [(NEAR, 0, 0, 0, down), (NEAR, 1, 1, 1, up), (NEXT, 0, 0, 1, down), (NEXT, 1, 1, 0, up),
            (FAR, 0, 2, 0, far), (FAR, 1, 2, 1, far)]
    for i, (one, two) in enumerate(routes):
        gather(ldx.at[i], mine[one], groups[one], 8 * i, send=False)
        tot = ldx[i, 0]
        for k in range(1, GROUP):
            tot = tot + ldx[i, k]
        ldz[i, pos[two]] = tot
        gather(ldz.at[i], pos[two], lines[two], 16 + 4 * i, wait=False)
    dcp = []
    for i, (blk, row, slot, h, d) in enumerate(dsrc):
        dcp.append(rc(28 + i, degs.at[blk, pl.ds(row, 1)], degr.at[slot, pl.ds(h, 1)], d))
        go(dcp[-1])
    for i, (one, two) in enumerate(routes):
        gather(ldz.at[i], pos[two], lines[two], 16 + 4 * i, send=False)
        tot = ldz[i, 0]
        for k in range(1, NZ):
            tot = tot + ldz[i, k]
        rsv[:, pl.ds(i * 2 * nl, 2 * nl)] = lax.rsqrt(tot)

    v0r.wait_recv()
    v3r.wait_recv()

    def product(blk, acc, r0=0, m=rows):
        part = None
        for s in range(4):
            for k in range(0, nl, 256):
                for w in range(k, k + 256, 128):
                    rv = jnp.broadcast_to(rsv[:, pl.ds(s * nl + w, 128)], (RC, 128))
                    for r in range(r0, r0 + m, RC):
                        scl[pl.ds(r, RC), pl.ds(w, 128)] = (kmat[blk, s, pl.ds(r, RC), pl.ds(w, 128)] * rv).astype(bf16)
                d = jnp.dot(scl[pl.ds(r0, m), pl.ds(k, 256)], evs[s, pl.ds(k, 256), :], preferred_element_type=f32)
                part = d if part is None else part + d
        acc[pl.ds(r0, m)] = part

    def send_part(n, h, d, k, add=None):
        v = acc[rq(2 * k + h)]
        if add is not None:
            v = v + precv[add, rq(k)].astype(f32)
        psend[n, rq(k)] = v.astype(psend.dtype)
        cp = rc(34 + 2 * n + k, psend.at[n, rq(k)], precv.at[n, rq(k)], d)
        go(cp)
        return cp

    first = []
    for k in range(2):
        product(FAR, acc, k * half, half)
        first.append((send_part(0, 0, up, k), send_part(1, 1, down, k)))
    product(NEAR, acc)
    last = [[send_part(2, 0, down, k), send_part(3, 1, up, k)] for k in range(2)]
    product(NEXT, acc)
    for k in range(2):
        first[k][0].wait_recv()
        last[k].append(send_part(4, 1, up, k, 0))
        first[k][1].wait_recv()
        last[k].append(send_part(5, 0, down, k, 1))
        if k == 0:
            product(OWN, acc2)

    nrows, nlands = float(NROWS), float(LANDMARKS)
    factor = (nrows * nlands) ** 0.5
    for cp in dcp:
        cp.wait_recv()
    inv = 1.0 / eigvals[...]
    cols = []
    for h in range(2):
        deg = degs[OWN, h:h + 1, :]
        for k in range(3):
            deg = deg + degr[k, h:h + 1, :]
        cols.append(jnp.broadcast_to(factor / jnp.sqrt(deg), (128, half)).T)
    for k in range(2):
        for cp in last[k]:
            cp.wait_recv()
        tops, lows = [], []
        for h in range(2):
            v = acc2[rq(2 * h + k)] + precv[2 + h, rq(k)].astype(f32) + precv[4 + h, rq(k)].astype(f32)
            col = cols[h][k * qr:(k + 1) * qr]
            v = jnp.concatenate([v[:, w:w + 128] * col for w in range(0, v.shape[1], 128)], axis=1) * inv
            coords[rq(2 * h + k)] = v
            tops.append(v.astype(bf16))
            lows.append((v - tops[-1].astype(f32)).astype(bf16))
        top, low = jnp.concatenate(tops, axis=0), jnp.concatenate(lows, axis=0)
        topt, lowt = top.T, low.T
        for i, (a, b) in enumerate(((0, 0), (0, 128), (128, 128))):
            v = jnp.dot(topt[a:a + 128], top[:, b:b + 128], preferred_element_type=f32)
            v = v + jnp.dot(topt[a:a + 128], low[:, b:b + 128], preferred_element_type=f32)
            v = v + jnp.dot(lowt[a:a + 128], top[:, b:b + 128], preferred_element_type=f32)
            v = v.reshape(gpart.shape[1:])
            gpart[i] = v if k == 0 else gpart[i] + v
    out_c = pltpu.make_async_copy(coords, coords_out, loc.at[3])
    out_c.start()
    for i in range(3):
        g = mine[i]
        for j, (p, d) in enumerate(groups[i]):
            go(pltpu.make_async_remote_copy(
                src_ref=gpart.at[i, p], dst_ref=grx.at[i, g], send_sem=gs.at[24 + 8 * i + j], recv_sem=gr.at[24 + 8 * i + g],
                device_id=d, device_id_type=pl.DeviceIdType.MESH))
    for i in range(3):
        two = (i + 1) % 3
        for p, d in groups[i]:
            pltpu.make_async_remote_copy(
                src_ref=gpart.at[i, p], dst_ref=grx.at[i, p], send_sem=gs.at[24 + 8 * i], recv_sem=gr.at[24 + 8 * i + p],
                device_id=d, device_id_type=pl.DeviceIdType.MESH).wait_recv()
        tot = gpart[i, mine[i]]
        for p, _ in groups[i]:
            tot = tot + grx[i, p]
        gry[i, pos[two]] = tot
        gather(gry.at[i], pos[two], lines[two], 48 + 4 * i, wait=False)
    for i in range(3):
        two, three = (i + 1) % 3, (i + 2) % 3
        gather(gry.at[i], pos[two], lines[two], 48 + 4 * i, send=False)
        tot = gry[i, 0]
        for k in range(1, NY):
            tot = tot + gry[i, k]
        grz[i, pos[three]] = tot
        gather(grz.at[i], pos[three], lines[three], 60 + 4 * i, wait=False)
    for i in range(3):
        three = (i + 2) % 3
        gather(grz.at[i], pos[three], lines[three], 60 + 4 * i, send=False)
        tot = grz[i, 0]
        for k in range(1, NZ):
            tot = tot + grz[i, k]
        gfull[i, mine[i]] = tot * (1.0 / NROWS)
        gather(gfull.at[i], mine[i], groups[i], 72 + 8 * i, wait=False)
    for i, (a, b) in enumerate(((0, 0), (0, 128), (128, 128))):
        gather(gfull.at[i], mine[i], groups[i], 72 + 8 * i, send=False)
        v = gfull[i].reshape(128, 128)
        gram[a:a + 128, b:b + 128] = v
        if a != b:
            gram[b:b + 128, a:a + 128] = v.T

    out_g = pltpu.make_async_copy(gram, gram_out, loc.at[4])
    out_g.start()
    for cp in sends:
        cp.wait_send()
    out_c.wait()
    out_g.wait()

def copy_out(c, g, c_out, g_out, c_buf, g_buf, sem):
    parts = [(c, c_buf, c_out, k) for k in range(4)] + [(g, g_buf, g_out, k) for k in range(2)]
    cin, cout = [], []
    for i, (src, buf, dst, k) in enumerate(parts):
        at = pl.ds(k * 128, 128)
        cin.append(pltpu.make_async_copy(src.at[at], buf.at[at], sem.at[2 * i]))
        cout.append(pltpu.make_async_copy(buf.at[at], dst.at[at], sem.at[2 * i + 1]))
        cin[-1].start()
    for a, b in zip(cin, cout):
        a.wait()
        b.start()
    for b in cout:
        b.wait()


NROWS, LANDMARKS = 65536, 16384


def per_device(items, landmarks, scales, eigvecs, eigvals):
    rows, dim = items.shape
    nl, width = eigvecs.shape
    half = rows // 2
    anyspec = pl.BlockSpec(memory_space=pl.ANY)
    vspec = pl.BlockSpec(memory_space=pltpu.VMEM)
    V, DMA = pltpu.VMEM, pltpu.SemaphoreType.DMA
    shapes = (jax.ShapeDtypeStruct((rows, width), f32), jax.ShapeDtypeStruct((width, width), f32))
    results = pl.pallas_call(
        kernel,
        out_shape=shapes,
        in_specs=[anyspec, anyspec, anyspec, vspec, vspec],
        out_specs=(anyspec, anyspec),
        scratch_shapes=[
            V((rows, width), f32), V((width, width), f32),
            V((4, rows, dim), bf16), V((4, nl, dim), bf16), V((4, nl, width), bf16), V((4, 8, nl), f32),
            V((4, rows, 128), f32), V((4, 4, rows, nl), f32), V((4, rows, 128), f32), V((4, 8, nl), f32),
            V((2, rows, NTILE), f32),
            V((2, GROUP, 1, 2 * nl), f32), V((2, NZ, 1, 2 * nl), f32), V((1, 4 * nl), f32), V((4, 2, half), f32), V((3, 2, half), f32),
            V((rows, nl), bf16), V((rows, width), f32), V((rows, width), f32), V((6, half, width), PT), V((6, half, width), PT),
            V((3, GROUP, 16, 128), f32), V((3, GROUP, 16, 128), f32), V((3, NY, 16, 128), f32), V((3, NZ, 16, 128), f32),
            V((3, GROUP, 16, 128), f32),
            DMA((5,)), DMA((46,)), DMA((46,)), DMA((96,)), DMA((96,)),
        ],
        compiler_params=pltpu.CompilerParams(collective_id=0, has_side_effects=True, vmem_limit_bytes=62 * 2**20),
    )(items, landmarks, eigvecs, scales.reshape(1, nl), eigvals.reshape(1, width))
    return pl.pallas_call(
        copy_out, out_shape=shapes, in_specs=[anyspec, anyspec], out_specs=(anyspec, anyspec),
        scratch_shapes=[V((rows, width), f32), V((width, width), f32), DMA((12,))])(*results)


def solution(mesh):
    return jax.shard_map(
        per_device, mesh=mesh,
        in_specs=(P(("dp", "land"), None), P("land", None), P("land"), P("land", None), P()),
        out_specs=(P(("dp", "land"), None), P()), check_vma=False)
```
